32 devices in a mesh: seq: 4 (over z), fsdp: 4 (over y, x), rep: 2 (over core).
Axes of the slice: x: 2, y: 2, z: 4, core: 2. Of those that a mesh axis runs over, the one named last changes fastest.
Arguments:
- tokens: bfloat16 [16, 1024, 2048], P(('fsdp', 'rep'), 'seq'), may hold values from -6 to 6
- cotangent: bfloat16 [16, 1024, 2048], P(('fsdp', 'rep'), 'seq'), may hold values from -6 to 6
- piece_start: int32 [16], P(('fsdp', 'rep')), may hold values from 0 to 768, as said below
- attention_gain: bfloat16 [2048], P('fsdp'), may hold values from 0.099609375 to 1.8984375
- query_weight: bfloat16 [2048, 2048], P('fsdp'), may hold values from -0.1875 to 0.1875
- key_weight: bfloat16 [2048, 2048], P('fsdp'), may hold values from -0.125 to 0.125
- value_weight: bfloat16 [2048, 2048], P('fsdp'), may hold values from -0.125 to 0.125
- output_weight: bfloat16 [2048, 2048], P('fsdp'), may hold values from -3 to 3
- feedforward_gain: bfloat16 [2048], P('fsdp'), may hold values from 0.099609375 to 1.8984375
- gate_weight: bfloat16 [2048, 8192], P('fsdp'), may hold values from -0.125 to 0.125
- up_weight: bfloat16 [2048, 8192], P('fsdp'), may hold values from -0.125 to 0.125
- down_weight: bfloat16 [8192, 2048], P('fsdp'), may hold values from -0.0625 to 0.0625
Outputs:
- layer_output: bfloat16 [16, 1024, 2048], P(('fsdp', 'rep'), 'seq')
- input_gradient: bfloat16 [16, 1024, 2048], P(('fsdp', 'rep'), 'seq')
- attention_gain_gradient: float32 [2048], P('fsdp')
- query_weight_gradient: float32 [2048, 2048], P('fsdp')
- key_weight_gradient: float32 [2048, 2048], P('fsdp')
- value_weight_gradient: float32 [2048, 2048], P('fsdp')
- output_weight_gradient: float32 [2048, 2048], P('fsdp')
- feedforward_gain_gradient: float32 [2048], P('fsdp')
- gate_weight_gradient: float32 [2048, 8192], P('fsdp')
- up_weight_gradient: float32 [2048, 8192], P('fsdp')
- down_weight_gradient: float32 [8192, 2048], P('fsdp')
The draws below stay inside these ranges and needn't reach their ends.
Inputs may be any that keep to these rules, and one draw needn't show every extreme that they name: `piece_start`: each sequence holds one picture piece of 256 positions starting here; in every draw some sequence starts it at 0 and some at 768.
All inputs are finite; a program needn't handle non-finite values.
Results may differ from the reference program's by a relative error of at most 0.02.
Values may be sent and summed in bfloat16 or wider, within the bound.
No kernel may reach another device: no remote copies, remote signals or barrier semaphores. Data moves between devices by JAX's collectives and lax.ppermute only.
A program may use at most 576 MiB of HBM per device.

```python
import jax
import jax.numpy as jnp
from jax import lax

D = 2048
HEADS = 32
HEAD_DIM = 64
FF = 8192
PIECE = 256
HEAD_GROUP = 8
SEQS = 16
LENGTH = 1024


def draw_piece_start(key, part):
    key_vals = jax.random.fold_in(key, 11)
    key_order = jax.random.fold_in(key, 23)
    highest = LENGTH - PIECE
    starts = jax.random.randint(key_vals, (SEQS,), 0, highest + 1, dtype=jnp.int32)
    order = jax.random.permutation(key_order, SEQS)
    starts = starts.at[order[0]].set(highest)
    starts = starts.at[order[1]].set(0)
    return starts.astype(jnp.int32)


def block_scale(rng, extent, pieces, least, high):
    level, own = 1.0, jax.random.fold_in(rng, 6)
    for dim, blocks in pieces:
        heights = jnp.exp(jax.random.uniform(jax.random.fold_in(own, dim), (blocks,), jnp.float32, least / len(pieces), high / len(pieces)))
        level = level * jnp.repeat(heights, extent[dim] // blocks).reshape([-1 if axis == dim else 1 for axis in range(len(extent))])
    return level


def bell_draw(rng, extent, deviation, bound, split=(), held_as=jnp.bfloat16):
    values = jax.random.normal(rng, extent, jnp.float32) * deviation
    if len(split) > 0:
        values = block_scale(rng, extent, split, -0.22, 0.18) * values
    return jnp.clip(values, min=-bound, max=bound).astype(held_as)


def setup_inputs(seed: int = 0) -> dict:
    key_list = jax.random.split(jax.random.key(seed), 13)
    tokens = bell_draw(key_list[0], (SEQS, LENGTH, D), 1.0, 6.0, ((0, 8), (1, 4)))
    cotangent = bell_draw(key_list[1], (SEQS, LENGTH, D), 1.0, 6.0, ((0, 8), (1, 4)))
    piece_start = draw_piece_start(jax.random.fold_in(key_list[12], 71), 0)
    attention_gain = jnp.clip(1.0 + 0.18 * jax.random.normal(key_list[3], (D,), jnp.float32), 0.099609375, 1.8984375).astype(jnp.bfloat16)
    query_weight = bell_draw(key_list[4], (D, D), (D // 2) ** -0.5, 0.1875, ((0, 4),))
    key_weight = bell_draw(key_list[5], (D, D), D ** -0.5, 0.125, ((0, 4),))
    value_weight = bell_draw(key_list[6], (D, D), D ** -0.5, 0.125, ((0, 4),))
    output_weight = bell_draw(key_list[7], (D, D), (max(D // 512, 1)) ** -0.5, 3.0, ((0, 4),))
    feedforward_gain = jnp.clip(1.0 + 0.18 * jax.random.normal(key_list[8], (D,), jnp.float32), 0.099609375, 1.8984375).astype(jnp.bfloat16)
    gate_weight = bell_draw(key_list[9], (D, FF), D ** -0.5, 0.125, ((0, 4),))
    up_weight = bell_draw(key_list[10], (D, FF), D ** -0.5, 0.125, ((0, 4),))
    down_weight = bell_draw(key_list[11], (FF, D), FF ** -0.5, 0.0625, ((0, 4),))
    return {"tokens": tokens, "cotangent": cotangent, "piece_start": piece_start, "attention_gain": attention_gain, "query_weight": query_weight, "key_weight": key_weight, "value_weight": value_weight, "output_weight": output_weight, "feedforward_gain": feedforward_gain, "gate_weight": gate_weight, "up_weight": up_weight, "down_weight": down_weight}


NORM_EPS = 1e-05
ROPE_BASE = 130000.0
MASKED_SCORE = -1e+30
HIGHEST_PREC = lax.Precision.HIGHEST

@jax.custom_vjp
def low(v):
    return lax.optimization_barrier(v.astype(jnp.bfloat16)).astype(jnp.float32)

@jax.custom_vjp
def low_back(v):
    return v

def low_keep(v):
    return (low(v), None)

def low_pass(kept, grad):
    return (grad,)

def back_keep(v):
    return (v, None)

def back_low(kept, grad):
    return (low(grad),)
low.defvjp(low_keep, low_pass)
low_back.defvjp(back_keep, back_low)

def product(left_op, right_op):
    return jnp.dot(left_op, right_op, precision=HIGHEST_PREC)

def normed(activation, gain_vec):
    scaling = lax.rsqrt(lax.optimization_barrier(jnp.mean(activation * activation, axis=-1, keepdims=True)) + NORM_EPS)
    return activation * scaling * gain_vec

def rotary(activation, offset):
    row_count = activation.shape[0]
    half_dim = HEAD_DIM // 2
    places = (offset + jnp.arange(row_count, dtype=jnp.int32)).astype(jnp.float32)
    frequency = ROPE_BASE ** (-jnp.arange(half_dim, dtype=jnp.float32) / half_dim)
    angles = places[:, None] * frequency[None, :]
    cosine = jnp.cos(angles)[:, None, :]
    sine_part = jnp.sin(angles)[:, None, :]
    per_head = activation.reshape(row_count, HEADS, HEAD_DIM)
    front_half = per_head[..., :half_dim]
    back_half = per_head[..., half_dim:]
    turned = jnp.concatenate([front_half * cosine - back_half * sine_part, back_half * cosine + front_half * sine_part], axis=-1)
    return turned.reshape(row_count, HEADS * HEAD_DIM)

def visible(query_pos, key_pos, piece_at):
    causal = key_pos[None, :] <= query_pos[:, None]
    query_in = (query_pos >= piece_at) & (query_pos < piece_at + PIECE)
    key_in = (key_pos >= piece_at) & (key_pos < piece_at + PIECE)
    return causal | query_in[:, None] & key_in[None, :]

def gated(gate_proj, up_proj):
    return jax.nn.silu(gate_proj) * up_proj

def head_block(triple, allowed):
    query_heads, key_heads, value_heads = triple
    scores = low_back(jnp.einsum('qhd,khd->hqk', query_heads, key_heads, precision=HIGHEST_PREC) * 0.125)
    scores = jnp.where(allowed[None], scores, MASKED_SCORE)
    row_max = lax.optimization_barrier(jnp.max(scores, axis=-1, keepdims=True))
    log_total = jnp.log(lax.optimization_barrier(jnp.sum(jnp.exp(scores - row_max), axis=-1, keepdims=True))) + row_max
    weights_soft = low(jnp.exp(scores - log_total))
    return jnp.einsum('hqk,khd->qhd', weights_soft, value_heads, precision=HIGHEST_PREC)

def layer(activation, piece_at, weights):
    attention_gain, query_weight, key_weight, value_weight, output_weight, feedforward_gain, gate_weight, up_weight, down_weight = weights
    length = activation.shape[0]
    features = activation.shape[1]
    positions = jnp.arange(length, dtype=jnp.int32)
    allowed = visible(positions, positions, piece_at)
    normed_first = low(normed(activation, attention_gain))
    queries = low(rotary(low_back(product(normed_first, query_weight)), 0))
    keys = low(rotary(low_back(product(normed_first, key_weight)), 0))
    values = low(low_back(product(normed_first, value_weight)))

    def head_split(stacked_in):
        return jnp.moveaxis(stacked_in.reshape(length, HEADS // HEAD_GROUP, HEAD_GROUP, HEAD_DIM), 1, 0)
    mixture = lax.map(jax.checkpoint(lambda triple: head_block(triple, allowed)), (head_split(queries), head_split(keys), head_split(values)))
    attended = low(low_back(jnp.moveaxis(mixture, 0, 1).reshape(length, features)))
    residual = activation + low_back(product(attended, output_weight))
    normed_second = low(normed(residual, feedforward_gain))
    gate_proj = low_back(product(normed_second, gate_weight))
    up_proj = low_back(product(normed_second, up_weight))
    inner_act = low(gated(gate_proj, up_proj))
    return residual + low_back(product(inner_act, down_weight))

def reference(tokens, cotangent, piece_start, attention_gain, query_weight, key_weight, value_weight, output_weight, feedforward_gain, gate_weight, up_weight, down_weight):
    floats = [array.astype(jnp.float32) for array in (tokens, attention_gain, query_weight, key_weight, value_weight, output_weight, feedforward_gain, gate_weight, up_weight, down_weight)]

    def forward(activations, *weights):

        def per_sequence(pair):
            return layer(pair[0], pair[1], weights)
        return lax.map(jax.checkpoint(per_sequence), (activations, piece_start))
    result, pullback = jax.vjp(forward, *floats)
    grads_all = pullback(cotangent.astype(jnp.float32))
    return (result.astype(jnp.bfloat16), grads_all[0].astype(jnp.bfloat16), grads_all[1], grads_all[2], grads_all[3], grads_all[4], grads_all[5], grads_all[6], grads_all[7], grads_all[8], grads_all[9])
```

```python
import functools
import math

import jax
import jax.numpy as jnp
from jax import lax
from jax.experimental import pallas as pl
from jax.experimental.pallas import tpu as pltpu
from jax.sharding import PartitionSpec as P

HEADS = 32
HEAD_DIM = 64
PIECE = 256
BLOCK = 256
LANES = 128

NORM_EPS = 1e-05
ROPE_BASE = 130000.0
MASKED_SCORE = -1e30
SCALE = 0.125 * math.log2(math.e)

bf16 = jnp.bfloat16
f32 = jnp.float32


def matmul(left_op, right_op, out=f32):
    return jnp.dot(left_op, right_op, preferred_element_type=f32).astype(out)


def outer_sum(left_op, right_op, out=f32):
    return lax.dot_general(
        left_op, right_op, (((0,), (0,)), ((), ())), preferred_element_type=f32
    ).astype(out)


def against(left_op, right_op, out=f32):
    return lax.dot_general(
        left_op, right_op, (((1,), (1,)), ((), ())), preferred_element_type=f32
    ).astype(out)


def dot_nt(left_op, right_op):
    return lax.dot_general(
        left_op, right_op, (((1,), (1,)), ((), ())), preferred_element_type=f32
    )


def dot_nn(left_op, right_op):
    return lax.dot_general(
        left_op, right_op, (((1,), (0,)), ((), ())), preferred_element_type=f32
    )


def lane_index(rows):
    return lax.broadcasted_iota(jnp.int32, (rows, LANES), 1)


def turned(value, cosine, sine):
    front = lax.rem(lane_index(value.shape[0]), HEAD_DIM) < HEAD_DIM // 2
    swapped = jnp.where(
        front,
        pltpu.roll(value, LANES - HEAD_DIM // 2, 1),
        pltpu.roll(value, HEAD_DIM // 2, 1),
    )
    return value * cosine + swapped * sine


def per_head_rows(value):
    first = lane_index(value.shape[0]) < HEAD_DIM
    zero = jnp.zeros_like(value)
    return jnp.concatenate([jnp.where(first, value, zero), jnp.where(first, zero, value)], axis=0)


def from_head_columns(value):
    rows = value.shape[1] // 2
    first = lax.broadcasted_iota(jnp.int32, (LANES, rows), 0) < HEAD_DIM
    return jnp.where(first, value[:, :rows], value[:, rows:]).T


def seen(key_block, query_block, start):
    key_pos = key_block * BLOCK + lax.broadcasted_iota(jnp.int32, (BLOCK, 2 * BLOCK), 0)
    query_pos = query_block * BLOCK + lax.rem(
        lax.broadcasted_iota(jnp.int32, (BLOCK, 2 * BLOCK), 1), BLOCK
    )
    key_in = (key_pos >= start) & (key_pos < start + PIECE)
    query_in = (query_pos >= start) & (query_pos < start + PIECE)
    return (key_pos <= query_pos) | (key_in & query_in)


def spills_over(query_block, start):
    return (start > query_block * BLOCK) & (start < (query_block + 1) * BLOCK)


def attend_forward_kernel(
    start_ref, lin_ref, cos_ref, sin_ref, out_ref, qkv_ref, lse_ref, s_ref, m_ref, l_ref, acc_ref
):
    start = start_ref[0]
    blocks = lin_ref.shape[0] // BLOCK
    for i in range(blocks):
        rows = slice(i * BLOCK, (i + 1) * BLOCK)
        cosine, sine = cos_ref[rows, :], sin_ref[rows, :]
        for part in range(2):
            columns = slice(part * LANES, (part + 1) * LANES)
            qkv_ref[rows, columns] = turned(lin_ref[rows, columns], cosine, sine).astype(bf16)
        qkv_ref[rows, 2 * LANES :] = lin_ref[rows, 2 * LANES :].astype(bf16)

    def key_rows(j):
        return qkv_ref[j * BLOCK : (j + 1) * BLOCK, LANES : 2 * LANES]

    def value_columns(j):
        return qkv_ref[j * BLOCK : (j + 1) * BLOCK, 2 * LANES :].T

    for i in range(blocks):
        rows = slice(i * BLOCK, (i + 1) * BLOCK)
        queries = per_head_rows(qkv_ref[rows, :LANES])
        over = spills_over(i, start)
        top = None
        for j in range(i + 1):
            scores = dot_nt(key_rows(j), queries)
            if j == i:
                scores = jnp.where(seen(j, i, start), scores, MASKED_SCORE)
            s_ref[j * BLOCK : (j + 1) * BLOCK, :] = scores
            best = jnp.max(scores, axis=0, keepdims=True)
            top = best if top is None else jnp.maximum(top, best)
        m_ref[...] = top

        if i + 1 < blocks:

            @pl.when(over)
            def _():
                scores = dot_nt(key_rows(i + 1), queries)
                scores = jnp.where(seen(i + 1, i, start), scores, MASKED_SCORE)
                s_ref[(i + 1) * BLOCK : (i + 2) * BLOCK, :] = scores
                m_ref[...] = jnp.maximum(m_ref[...], jnp.max(scores, axis=0, keepdims=True))

        top = m_ref[...]
        shift = top * SCALE
        total, mixed = None, None
        for j in range(i + 1):
            weights = jnp.exp2(s_ref[j * BLOCK : (j + 1) * BLOCK, :] * SCALE - shift)
            part_total = jnp.sum(weights, axis=0, keepdims=True)
            part_mixed = dot_nn(value_columns(j), weights.astype(bf16))
            total = part_total if total is None else total + part_total
            mixed = part_mixed if mixed is None else mixed + part_mixed
        l_ref[...] = total
        acc_ref[...] = mixed

        if i + 1 < blocks:

            @pl.when(over)
            def _():
                weights = jnp.exp2(s_ref[(i + 1) * BLOCK : (i + 2) * BLOCK, :] * SCALE - shift)
                l_ref[...] += jnp.sum(weights, axis=0, keepdims=True)
                acc_ref[...] += dot_nn(value_columns(i + 1), weights.astype(bf16))

        total = l_ref[...]
        out_ref[rows, :] = from_head_columns(acc_ref[...] / total).astype(bf16)
        lse_ref[0, i : i + 1, :] = shift + jnp.log2(total)


def attend_backward_kernel(
    start_ref, qkv_ref, out_ref, grad_ref, lse_ref, cos_ref, sin_ref, lin_ref, dq_ref, dk_ref, dv_ref
):
    start = start_ref[0]
    blocks = qkv_ref.shape[0] // BLOCK
    dk_ref[...] = jnp.zeros_like(dk_ref)
    dv_ref[...] = jnp.zeros_like(dv_ref)
    for i in range(blocks):
        rows = slice(i * BLOCK, (i + 1) * BLOCK)
        queries = per_head_rows(qkv_ref[rows, :LANES])
        grads_in = grad_ref[rows, :]
        grads = per_head_rows(grads_in)
        both = (grads_in.astype(f32) * out_ref[rows, :].astype(f32)).T
        delta = jnp.concatenate(
            [
                jnp.sum(both[:HEAD_DIM], axis=0, keepdims=True),
                jnp.sum(both[HEAD_DIM:], axis=0, keepdims=True),
            ],
            axis=1,
        )
        lse = lse_ref[0, i : i + 1, :]

        def one(j, masked):
            keys_at = slice(j * BLOCK, (j + 1) * BLOCK)
            keys = qkv_ref[keys_at, LANES : 2 * LANES]
            scores = dot_nt(keys, queries)
            weights = jnp.exp2(scores * SCALE - lse)
            if masked:
                weights = jnp.where(seen(j, i, start), weights, 0.0)
            weight_grads = dot_nt(qkv_ref[keys_at, 2 * LANES :], grads)
            score_grads = (weights * (weight_grads - delta)).astype(bf16)
            dv_ref[keys_at, :] += dot_nn(weights.astype(bf16), grads)
            dk_ref[keys_at, :] += dot_nn(score_grads, queries)
            return dot_nn(keys.T, score_grads)

        query_grads = None
        for j in range(i + 1):
            part = one(j, j == i)
            query_grads = part if query_grads is None else query_grads + part
        dq_ref[...] = query_grads

        if i + 1 < blocks:

            @pl.when(spills_over(i, start))
            def _():
                dq_ref[...] += one(i + 1, True)

        lin_ref[rows, :LANES] = turned(
            from_head_columns(dq_ref[...]) * 0.125, cos_ref[rows, :], -sin_ref[rows, :]
        ).astype(bf16)
    for i in range(blocks):
        rows = slice(i * BLOCK, (i + 1) * BLOCK)
        lin_ref[rows, LANES : 2 * LANES] = turned(
            dk_ref[rows, :] * 0.125, cos_ref[rows, :], -sin_ref[rows, :]
        ).astype(bf16)
        lin_ref[rows, 2 * LANES :] = dv_ref[rows, :].astype(bf16)


def column_block(length, width):
    return pl.BlockSpec((length, width), lambda p, s: (0, p))


def whole_block(shape):
    return pl.BlockSpec(shape, lambda p, s: (0,) * len(shape))


def attend_forward(start, lin, cosine, sine):
    length, width = lin.shape
    pairs = width // (3 * LANES)
    blocks = length // BLOCK
    flops = pairs * 2 * 2 * 2 * length * length * LANES
    return pl.pallas_call(
        attend_forward_kernel,
        grid_spec=pltpu.PrefetchScalarGridSpec(
            num_scalar_prefetch=1,
            grid=(pairs,),
            in_specs=[
                column_block(length, 3 * LANES),
                whole_block((length, LANES)),
                whole_block((length, LANES)),
            ],
            out_specs=[
                column_block(length, LANES),
                column_block(length, 3 * LANES),
                pl.BlockSpec((1, blocks, 2 * BLOCK), lambda p, s: (p, 0, 0)),
            ],
            scratch_shapes=[
                pltpu.VMEM((length, 2 * BLOCK), f32),
                pltpu.VMEM((1, 2 * BLOCK), f32),
                pltpu.VMEM((1, 2 * BLOCK), f32),
                pltpu.VMEM((LANES, 2 * BLOCK), f32),
            ],
        ),
        out_shape=[
            jax.ShapeDtypeStruct((length, pairs * LANES), bf16),
            jax.ShapeDtypeStruct((length, width), bf16),
            jax.ShapeDtypeStruct((pairs, blocks, 2 * BLOCK), f32),
        ],
        cost_estimate=pl.CostEstimate(
            flops=flops,
            bytes_accessed=length * width * 6 + length * pairs * LANES * 2,
            transcendentals=pairs * 2 * length * length // 2,
        ),
        name="attend_forward",
    )(start, lin, cosine, sine)


def attend_backward(start, qkv, out, grad, lse, cosine, sine):
    length, width = qkv.shape
    pairs = width // (3 * LANES)
    blocks = length // BLOCK
    flops = pairs * 2 * 5 * 2 * length * length * LANES
    return pl.pallas_call(
        attend_backward_kernel,
        grid_spec=pltpu.PrefetchScalarGridSpec(
            num_scalar_prefetch=1,
            grid=(pairs,),
            in_specs=[
                column_block(length, 3 * LANES),
                column_block(length, LANES),
                column_block(length, LANES),
                pl.BlockSpec((1, blocks, 2 * BLOCK), lambda p, s: (p, 0, 0)),
                whole_block((length, LANES)),
                whole_block((length, LANES)),
            ],
            out_specs=column_block(length, 3 * LANES),
            scratch_shapes=[
                pltpu.VMEM((LANES, 2 * BLOCK), f32),
                pltpu.VMEM((length, LANES), f32),
                pltpu.VMEM((length, LANES), f32),
            ],
        ),
        out_shape=jax.ShapeDtypeStruct((length, width), bf16),
        cost_estimate=pl.CostEstimate(
            flops=flops,
            bytes_accessed=length * width * 4 + length * pairs * LANES * 4,
            transcendentals=pairs * 2 * length * length // 2,
        ),
        name="attend_backward",
    )(start, qkv, out, grad, lse, cosine, sine)


def swap(value, axis, size, distance):
    return lax.ppermute(value, axis, [(i, i ^ distance) for i in range(size)])


def bit_orders(size):
    bits = [1 << b for b in range(size.bit_length() - 1)]
    return bits, bits[::-1]


def gather_rows(value, axis, size):
    half = value.shape[0] // 2
    parts = []
    for part, order in zip((value[:half], value[half:]), bit_orders(size)):
        held = {0: part}
        for bit in order:
            for d in list(held):
                held[d ^ bit] = swap(held[d], axis, size, bit)
        parts.append(held)
    return jnp.concatenate([parts[h][d] for d in range(size) for h in range(2)], axis=0)


def scatter_rows(block_of, axis, size):
    blocks = {d: block_of(d) for d in range(size)}
    half = blocks[0].shape[0] // 2
    sums = []
    for h, order in enumerate(bit_orders(size)):
        held = {d: b[h * half : (h + 1) * half] for d, b in blocks.items()}
        for bit in order:
            for d in [d for d in held if d & bit]:
                came = swap(held.pop(d).astype(bf16), axis, size, bit)
                held[d ^ bit] = held[d ^ bit].astype(f32) + came.astype(f32)
        sums.append(held[0])
    return jnp.concatenate(sums, axis=0)


def local(
    tokens,
    cotangent,
    piece_start,
    attention_gain,
    query_weight,
    key_weight,
    value_weight,
    output_weight,
    feedforward_gain,
    gate_weight,
    up_weight,
    down_weight,
):
    lengths, shards, copies = (lax.axis_size(name) for name in ("seq", "fsdp", "rep"))
    batch, span, features = tokens.shape
    hidden = gate_weight.shape[1]
    team = lengths // batch
    members = lengths * copies
    everyone = ("seq", "rep")
    own_rows = batch * span
    length = lengths * span
    part = hidden // shards
    rows = features // shards
    heads_width = features // (shards * team)
    width = features // team
    z, f, r = (lax.axis_index(name) for name in ("seq", "fsdp", "rep"))
    line = z * copies + r
    mine = lax.rem(line, team)
    local_seq = lax.rem(line // team, batch)

    def perm_in(k):
        pairs = []
        for zz in range(lengths):
            for rr in range(copies):
                j = (zz + k) % batch
                pairs.append((zz * copies + rr, (rr * batch + j) * team + zz // batch))
        return pairs

    def take_sequence(value):
        came = [
            lax.ppermute(
                lax.dynamic_index_in_dim(value, lax.rem(z + k, batch), 0, False),
                everyone,
                perm_in(k),
            )
            for k in range(batch)
        ]
        return jnp.concatenate(
            [lax.select_n(lax.rem(local_seq + batch - b, batch), *came) for b in range(batch)],
            axis=0,
        )

    def give_back(value):
        blocks = value.reshape(batch, span, features)
        came = [
            lax.ppermute(
                lax.dynamic_index_in_dim(blocks, lax.rem(local_seq + batch - k, batch), 0, False),
                everyone,
                [(b, a) for a, b in perm_in(k)],
            )
            for k in range(batch)
        ]
        return jnp.stack(
            [lax.select_n(lax.rem(j + batch * lengths - z, batch), *came) for j in range(batch)]
        )

    def team_gather(value):
        came = [value] + [swap(value, everyone, members, d) for d in range(1, team)]
        return jnp.concatenate([lax.select_n(mine ^ u, *came) for u in range(team)], axis=0)

    def team_scatter(value):
        def block(d):
            return lax.dynamic_slice_in_dim(value, (mine ^ d) * own_rows, own_rows, 0)

        total = block(0).astype(f32)
        for d in range(1, team):
            total = total + swap(block(d), everyone, members, d).astype(f32)
        return total

    def shard_gather_small(value):
        out = jnp.zeros((shards,) + value.shape, value.dtype)
        for d in range(shards):
            came = swap(value, "fsdp", shards, d) if d else value
            out = lax.dynamic_update_index_in_dim(out, came, f ^ d, 0)
        return out

    def head_columns(weight):
        split = weight.reshape(weight.shape[0], shards, team, heads_width)
        return lax.dynamic_index_in_dim(split, mine, 2, False).reshape(weight.shape[0], width)

    tokens_own = take_sequence(tokens)
    start = lax.ppermute(
        lax.dynamic_index_in_dim(piece_start, lax.rem(z, batch), 0), everyone, perm_in(0)
    )

    pairs = width // LANES
    wqkv_rows = jnp.stack(
        [
            head_columns(w).reshape(rows, pairs, LANES)
            for w in (query_weight, key_weight, value_weight)
        ],
        axis=2,
    ).reshape(rows, 3 * width)
    wqkv = lax.all_gather(wqkv_rows, "fsdp", axis=0, tiled=True)
    wo_rows = lax.dynamic_slice_in_dim(output_weight, mine * heads_width, heads_width, 0)
    wo = lax.all_gather(wo_rows, "fsdp", axis=0, tiled=True)

    gains = shard_gather_small(jnp.stack([attention_gain, feedforward_gain]))
    gain_first = gains[:, 0].reshape(features).astype(f32)
    gain_second = gains[:, 1].reshape(features).astype(f32)

    half_dim = HEAD_DIM // 2
    places = jnp.arange(length, dtype=jnp.int32).astype(f32)
    frequency = ROPE_BASE ** (-jnp.arange(half_dim, dtype=f32) / half_dim)
    angles = places[:, None] * frequency[None, :]
    cos_half, sin_half = jnp.cos(angles), jnp.sin(angles)
    cosine = jnp.concatenate([cos_half] * 4, axis=1)
    sine = jnp.concatenate([-sin_half, sin_half] * 2, axis=1)

    activation = tokens_own.astype(f32)
    scale_first = lax.rsqrt(jnp.mean(activation * activation, axis=-1, keepdims=True) + NORM_EPS)
    first_own = (activation * scale_first * gain_first).astype(bf16)
    first = team_gather(first_own)
    lin = matmul(first, wqkv)
    attended, qkv, lse = attend_forward(start, lin, cosine, sine)
    residual = activation + team_scatter(matmul(attended, wo, bf16))
    scale_second = lax.rsqrt(jnp.mean(residual * residual, axis=-1, keepdims=True) + NORM_EPS)
    second_own = (residual * scale_second * gain_second).astype(bf16)

    slab = part // copies

    def hidden_columns(weight):
        out = jnp.zeros((shards, rows, slab), bf16)
        for d in range(shards):
            piece = lax.dynamic_slice_in_dim(weight, (f ^ d) * part + r * slab, slab, 1)
            came = swap(piece, "fsdp", shards, d) if d else piece
            out = lax.dynamic_update_index_in_dim(out, came, f ^ d, 0)
        out = out.reshape(features, slab)
        came = [out] + [swap(out, "rep", copies, d) for d in range(1, copies)]
        return jnp.concatenate([lax.select_n(r ^ u, *came) for u in range(copies)], axis=1)

    gate_w = hidden_columns(gate_weight)
    up_w = hidden_columns(up_weight)

    cotangent_own = take_sequence(cotangent)
    cot = gather_rows(cotangent_own, "fsdp", shards)
    second = gather_rows(second_own, "fsdp", shards)

    gate = matmul(second, gate_w)
    up = matmul(second, up_w)
    inner_grad = against(cot, down_weight)
    sig = jax.nn.sigmoid(gate)
    silu = gate * sig
    inner = (silu * up).astype(bf16)
    gate_grad = (inner_grad * up * (sig * (1.0 + gate * (1.0 - sig)))).astype(bf16)
    up_grad = (inner_grad * silu).astype(bf16)

    second_grad_part = (against(gate_grad, gate_w) + against(up_grad, up_w)).astype(bf16)
    second_grad = scatter_rows(
        lambda d: second_grad_part[d * own_rows : (d + 1) * own_rows], "fsdp", shards
    )
    down_part = matmul(inner, down_weight, bf16)
    layer_rows = residual + scatter_rows(
        lambda d: down_part[d * own_rows : (d + 1) * own_rows], "fsdp", shards
    )
    layer_output = give_back(layer_rows.astype(bf16))

    down_term = outer_sum(inner, cot, bf16)
    down_grad = lax.psum(down_term, everyone).astype(f32)

    tiny = rows // members

    def reorder(term):
        return term.reshape(shards, members, tiny, part).transpose(1, 0, 2, 3)

    gate_up_term = jnp.stack(
        [reorder(outer_sum(second, gate_grad, bf16)), reorder(outer_sum(second, up_grad, bf16))],
        axis=1,
    )
    gate_up_piece = lax.psum_scatter(gate_up_term, everyone, scatter_dimension=0, tiled=False)
    spread = jnp.zeros_like(gate_up_piece)
    for d in range(shards):
        piece = lax.dynamic_index_in_dim(gate_up_piece, f ^ d, 1, False)
        came = swap(piece, "fsdp", shards, d) if d else piece
        spread = lax.dynamic_update_index_in_dim(spread, came, f ^ d, 1)
    gate_up_all = lax.all_gather(spread, everyone, axis=0, tiled=False)
    gate_grad_w, up_grad_w = (
        gate_up_all[:, i].transpose(0, 2, 1, 3).reshape(rows, hidden).astype(f32) for i in range(2)
    )

    output_rows = cotangent_own.astype(f32)
    scaled = second_grad * gain_second
    residual_grad = (
        output_rows
        + scale_second * scaled
        - residual
        * (scale_second * scale_second * scale_second)
        * jnp.mean(scaled * residual, axis=-1, keepdims=True)
    )
    gain_second_term = jnp.sum(second_grad * residual * scale_second, axis=0)
    branch_own = residual_grad.astype(bf16)
    branch = team_gather(branch_own)

    attended_grad = against(branch, wo, bf16)
    wo_term = outer_sum(attended, branch, bf16)
    lin_grad = attend_backward(start, qkv, attended, attended_grad, lse, cosine, sine)
    first_grad = team_scatter(against(lin_grad, wqkv, bf16))
    wqkv_term = outer_sum(first, lin_grad, bf16)

    scaled = first_grad * gain_first
    input_rows = (
        residual_grad
        + scale_first * scaled
        - activation
        * (scale_first * scale_first * scale_first)
        * jnp.mean(scaled * activation, axis=-1, keepdims=True)
    )
    gain_first_term = jnp.sum(first_grad * activation * scale_first, axis=0)
    input_gradient = give_back(input_rows.astype(bf16))

    def weight_rows(term):
        size = term.shape[0] // shards

        def block(d):
            return lax.dynamic_slice_in_dim(term, (f ^ d) * size, size, 0)

        return scatter_rows(block, "fsdp", shards).astype(bf16)

    stride = team // copies
    if stride == 1:
        same_heads = None
    else:
        same_heads = [list(range(i, lengths, stride)) for i in range(stride)]
    wqkv_sum, wo_sum = (
        lax.psum(weight_rows(term), "seq", axis_index_groups=same_heads)
        for term in (wqkv_term, wo_term)
    )

    def team_stack(value):
        came = [value] + [swap(value, everyone, members, d) for d in range(1, team)]
        return [lax.select_n(mine ^ u, *came) for u in range(team)]

    wqkv_all = [v.reshape(rows, pairs, 3, LANES) for v in team_stack(wqkv_sum)]
    output_grad_w = jnp.concatenate(team_stack(wo_sum), axis=0).astype(f32)

    def head_gradient(i):
        split = [v[:, :, i].reshape(rows, shards, heads_width) for v in wqkv_all]
        return jnp.stack(split, axis=2).reshape(rows, features).astype(f32)

    gain_terms = lax.psum(jnp.stack([gain_first_term, gain_second_term]), ("seq", "fsdp", "rep"))
    gain_grads = lax.dynamic_slice_in_dim(gain_terms, f * rows, rows, 1)
    return (
        layer_output,
        input_gradient,
        gain_grads[0],
        head_gradient(0),
        head_gradient(1),
        head_gradient(2),
        output_grad_w,
        gain_grads[1],
        gate_grad_w,
        up_grad_w,
        down_grad,
    )


def solution(mesh):
    placed = (
        P(("fsdp", "rep"), "seq", None),
        P(("fsdp", "rep"), "seq", None),
        P(("fsdp", "rep")),
        P("fsdp"),
        P("fsdp", None),
        P("fsdp", None),
        P("fsdp", None),
        P("fsdp", None),
        P("fsdp"),
        P("fsdp", None),
        P("fsdp", None),
        P("fsdp", None),
    )
    return jax.shard_map(
        local,
        mesh=mesh,
        in_specs=placed,
        out_specs=(
            P(("fsdp", "rep"), "seq", None),
            P(("fsdp", "rep"), "seq", None),
            P("fsdp"),
            P("fsdp", None),
            P("fsdp", None),
            P("fsdp", None),
            P("fsdp", None),
            P("fsdp"),
            P("fsdp", None),
            P("fsdp", None),
            P("fsdp", None),
        ),
        check_vma=False,
    )
```

```python
import functools
import math

import jax
import jax.numpy as jnp
from jax import lax
from jax.experimental import pallas as pl
from jax.experimental.pallas import tpu as pltpu
from jax.sharding import PartitionSpec as P

HEADS = 32
HEAD_DIM = 64
PIECE = 256
BLOCK = 256
LANES = 128

NORM_EPS = 1e-05
ROPE_BASE = 130000.0
MASKED_SCORE = -1e30
SCALE = 0.125 * math.log2(math.e)

bf16 = jnp.bfloat16
f32 = jnp.float32


def matmul(left_op, right_op, out=f32):
    return jnp.dot(left_op, right_op, preferred_element_type=f32).astype(out)


def outer_sum(left_op, right_op, out=f32):
    return lax.dot_general(
        left_op, right_op, (((0,), (0,)), ((), ())), preferred_element_type=f32
    ).astype(out)


def against(left_op, right_op, out=f32):
    return lax.dot_general(
        left_op, right_op, (((1,), (1,)), ((), ())), preferred_element_type=f32
    ).astype(out)


def dot_nt(left_op, right_op):
    return lax.dot_general(
        left_op, right_op, (((1,), (1,)), ((), ())), preferred_element_type=f32
    )


def dot_nn(left_op, right_op):
    return lax.dot_general(
        left_op, right_op, (((1,), (0,)), ((), ())), preferred_element_type=f32
    )


def lane_index(rows):
    return lax.broadcasted_iota(jnp.int32, (rows, LANES), 1)


def turned(value, cosine, sine):
    front = lax.rem(lane_index(value.shape[0]), HEAD_DIM) < HEAD_DIM // 2
    swapped = jnp.where(
        front,
        pltpu.roll(value, LANES - HEAD_DIM // 2, 1),
        pltpu.roll(value, HEAD_DIM // 2, 1),
    )
    return value * cosine + swapped * sine


def per_head_rows(value):
    first = lane_index(value.shape[0]) < HEAD_DIM
    zero = jnp.zeros_like(value)
    return jnp.concatenate([jnp.where(first, value, zero), jnp.where(first, zero, value)], axis=0)


def from_head_columns(value):
    rows = value.shape[1] // 2
    first = lax.broadcasted_iota(jnp.int32, (LANES, rows), 0) < HEAD_DIM
    return jnp.where(first, value[:, :rows], value[:, rows:]).T


def seen(key_block, query_block, start):
    key_pos = key_block * BLOCK + lax.broadcasted_iota(jnp.int32, (BLOCK, 2 * BLOCK), 0)
    query_pos = query_block * BLOCK + lax.rem(
        lax.broadcasted_iota(jnp.int32, (BLOCK, 2 * BLOCK), 1), BLOCK
    )
    key_in = (key_pos >= start) & (key_pos < start + PIECE)
    query_in = (query_pos >= start) & (query_pos < start + PIECE)
    return (key_pos <= query_pos) | (key_in & query_in)


def spills_over(query_block, start):
    return (start > query_block * BLOCK) & (start < (query_block + 1) * BLOCK)


def attend_forward_kernel(
    start_ref, lin_ref, cos_ref, sin_ref, out_ref, qkv_ref, lse_ref, s_ref, m_ref, l_ref, acc_ref
):
    start = start_ref[0]
    blocks = lin_ref.shape[0] // BLOCK
    for i in range(blocks):
        rows = slice(i * BLOCK, (i + 1) * BLOCK)
        cosine, sine = cos_ref[rows, :], sin_ref[rows, :]
        for part in range(2):
            columns = slice(part * LANES, (part + 1) * LANES)
            qkv_ref[rows, columns] = turned(lin_ref[rows, columns], cosine, sine).astype(bf16)
        qkv_ref[rows, 2 * LANES :] = lin_ref[rows, 2 * LANES :].astype(bf16)

    def key_rows(j):
        return qkv_ref[j * BLOCK : (j + 1) * BLOCK, LANES : 2 * LANES]

    def value_columns(j):
        return qkv_ref[j * BLOCK : (j + 1) * BLOCK, 2 * LANES :].T

    for i in range(blocks):
        rows = slice(i * BLOCK, (i + 1) * BLOCK)
        queries = per_head_rows(qkv_ref[rows, :LANES])
        over = spills_over(i, start)
        top = None
        for j in range(i + 1):
            scores = dot_nt(key_rows(j), queries)
            if j == i:
                scores = jnp.where(seen(j, i, start), scores, MASKED_SCORE)
            s_ref[j * BLOCK : (j + 1) * BLOCK, :] = scores
            best = jnp.max(scores, axis=0, keepdims=True)
            top = best if top is None else jnp.maximum(top, best)
        m_ref[...] = top

        if i + 1 < blocks:

            @pl.when(over)
            def _():
                scores = dot_nt(key_rows(i + 1), queries)
                scores = jnp.where(seen(i + 1, i, start), scores, MASKED_SCORE)
                s_ref[(i + 1) * BLOCK : (i + 2) * BLOCK, :] = scores
                m_ref[...] = jnp.maximum(m_ref[...], jnp.max(scores, axis=0, keepdims=True))

        top = m_ref[...]
        shift = top * SCALE
        total, mixed = None, None
        for j in range(i + 1):
            weights = jnp.exp2(s_ref[j * BLOCK : (j + 1) * BLOCK, :] * SCALE - shift)
            part_total = jnp.sum(weights, axis=0, keepdims=True)
            part_mixed = dot_nn(value_columns(j), weights.astype(bf16))
            total = part_total if total is None else total + part_total
            mixed = part_mixed if mixed is None else mixed + part_mixed
        l_ref[...] = total
        acc_ref[...] = mixed

        if i + 1 < blocks:

            @pl.when(over)
            def _():
                weights = jnp.exp2(s_ref[(i + 1) * BLOCK : (i + 2) * BLOCK, :] * SCALE - shift)
                l_ref[...] += jnp.sum(weights, axis=0, keepdims=True)
                acc_ref[...] += dot_nn(value_columns(i + 1), weights.astype(bf16))

        total = l_ref[...]
        out_ref[rows, :] = from_head_columns(acc_ref[...] / total).astype(bf16)
        lse_ref[0, i : i + 1, :] = shift + jnp.log2(total)


def attend_backward_kernel(
    start_ref, qkv_ref, out_ref, grad_ref, lse_ref, cos_ref, sin_ref, lin_ref, dq_ref, dk_ref, dv_ref
):
    start = start_ref[0]
    blocks = qkv_ref.shape[0] // BLOCK
    dk_ref[...] = jnp.zeros_like(dk_ref)
    dv_ref[...] = jnp.zeros_like(dv_ref)
    for i in range(blocks):
        rows = slice(i * BLOCK, (i + 1) * BLOCK)
        queries = per_head_rows(qkv_ref[rows, :LANES])
        grads_in = grad_ref[rows, :]
        grads = per_head_rows(grads_in)
        both = (grads_in.astype(f32) * out_ref[rows, :].astype(f32)).T
        delta = jnp.concatenate(
            [
                jnp.sum(both[:HEAD_DIM], axis=0, keepdims=True),
                jnp.sum(both[HEAD_DIM:], axis=0, keepdims=True),
            ],
            axis=1,
        )
        lse = lse_ref[0, i : i + 1, :]

        def one(j, masked):
            keys_at = slice(j * BLOCK, (j + 1) * BLOCK)
            keys = qkv_ref[keys_at, LANES : 2 * LANES]
            scores = dot_nt(keys, queries)
            weights = jnp.exp2(scores * SCALE - lse)
            if masked:
                weights = jnp.where(seen(j, i, start), weights, 0.0)
            weight_grads = dot_nt(qkv_ref[keys_at, 2 * LANES :], grads)
            score_grads = (weights * (weight_grads - delta)).astype(bf16)
            dv_ref[keys_at, :] += dot_nn(weights.astype(bf16), grads)
            dk_ref[keys_at, :] += dot_nn(score_grads, queries)
            return dot_nn(keys.T, score_grads)

        query_grads = None
        for j in range(i + 1):
            part = one(j, j == i)
            query_grads = part if query_grads is None else query_grads + part
        dq_ref[...] = query_grads

        if i + 1 < blocks:

            @pl.when(spills_over(i, start))
            def _():
                dq_ref[...] += one(i + 1, True)

        lin_ref[rows, :LANES] = turned(
            from_head_columns(dq_ref[...]) * 0.125, cos_ref[rows, :], -sin_ref[rows, :]
        ).astype(bf16)
    for i in range(blocks):
        rows = slice(i * BLOCK, (i + 1) * BLOCK)
        lin_ref[rows, LANES : 2 * LANES] = turned(
            dk_ref[rows, :] * 0.125, cos_ref[rows, :], -sin_ref[rows, :]
        ).astype(bf16)
        lin_ref[rows, 2 * LANES :] = dv_ref[rows, :].astype(bf16)


def column_block(length, width):
    return pl.BlockSpec((length, width), lambda p, s: (0, p))


def whole_block(shape):
    return pl.BlockSpec(shape, lambda p, s: (0,) * len(shape))


def attend_forward(start, lin, cosine, sine):
    length, width = lin.shape
    pairs = width // (3 * LANES)
    blocks = length // BLOCK
    flops = pairs * 2 * 2 * 2 * length * length * LANES
    return pl.pallas_call(
        attend_forward_kernel,
        grid_spec=pltpu.PrefetchScalarGridSpec(
            num_scalar_prefetch=1,
            grid=(pairs,),
            in_specs=[
                column_block(length, 3 * LANES),
                whole_block((length, LANES)),
                whole_block((length, LANES)),
            ],
            out_specs=[
                column_block(length, LANES),
                column_block(length, 3 * LANES),
                pl.BlockSpec((1, blocks, 2 * BLOCK), lambda p, s: (p, 0, 0)),
            ],
            scratch_shapes=[
                pltpu.VMEM((length, 2 * BLOCK), f32),
                pltpu.VMEM((1, 2 * BLOCK), f32),
                pltpu.VMEM((1, 2 * BLOCK), f32),
                pltpu.VMEM((LANES, 2 * BLOCK), f32),
            ],
        ),
        out_shape=[
            jax.ShapeDtypeStruct((length, pairs * LANES), bf16),
            jax.ShapeDtypeStruct((length, width), bf16),
            jax.ShapeDtypeStruct((pairs, blocks, 2 * BLOCK), f32),
        ],
        cost_estimate=pl.CostEstimate(
            flops=flops,
            bytes_accessed=length * width * 6 + length * pairs * LANES * 2,
            transcendentals=pairs * 2 * length * length // 2,
        ),
        name="attend_forward",
    )(start, lin, cosine, sine)


def attend_backward(start, qkv, out, grad, lse, cosine, sine):
    length, width = qkv.shape
    pairs = width // (3 * LANES)
    blocks = length // BLOCK
    flops = pairs * 2 * 5 * 2 * length * length * LANES
    return pl.pallas_call(
        attend_backward_kernel,
        grid_spec=pltpu.PrefetchScalarGridSpec(
            num_scalar_prefetch=1,
            grid=(pairs,),
            in_specs=[
                column_block(length, 3 * LANES),
                column_block(length, LANES),
                column_block(length, LANES),
                pl.BlockSpec((1, blocks, 2 * BLOCK), lambda p, s: (p, 0, 0)),
                whole_block((length, LANES)),
                whole_block((length, LANES)),
            ],
            out_specs=column_block(length, 3 * LANES),
            scratch_shapes=[
                pltpu.VMEM((LANES, 2 * BLOCK), f32),
                pltpu.VMEM((length, LANES), f32),
                pltpu.VMEM((length, LANES), f32),
            ],
        ),
        out_shape=jax.ShapeDtypeStruct((length, width), bf16),
        cost_estimate=pl.CostEstimate(
            flops=flops,
            bytes_accessed=length * width * 4 + length * pairs * LANES * 4,
            transcendentals=pairs * 2 * length * length // 2,
        ),
        name="attend_backward",
    )(start, qkv, out, grad, lse, cosine, sine)


def widen_kernel(place_ref, mine_ref, other_ref, out_ref):
    own = pl.program_id(0) == place_ref[0]

    @pl.when(own)
    def _():
        out_ref[...] = mine_ref[...].astype(f32)

    @pl.when(jnp.logical_not(own))
    def _():
        out_ref[...] = other_ref[...].astype(f32)


def widen_halves(place, mine, other):
    rows, width = mine.shape
    block = rows
    while block * width > 512 * 1024 and block % 32 == 0:
        block //= 2
    steps = rows // block
    return pl.pallas_call(
        widen_kernel,
        grid_spec=pltpu.PrefetchScalarGridSpec(
            num_scalar_prefetch=1,
            grid=(2, steps),
            in_specs=[
                pl.BlockSpec((block, width), lambda u, i, p: (jnp.where(u == p[0], i, 0), 0)),
                pl.BlockSpec((block, width), lambda u, i, p: (jnp.where(u == p[0], 0, i), 0)),
            ],
            out_specs=pl.BlockSpec((block, width), lambda u, i, p: (u * steps + i, 0)),
        ),
        out_shape=jax.ShapeDtypeStruct((2 * rows, width), f32),
        cost_estimate=pl.CostEstimate(
            flops=0, bytes_accessed=12 * rows * width, transcendentals=0
        ),
        name="widen_halves",
    )(place, mine, other)


def spread_heads_kernel(place_ref, mine_ref, other_ref, q_ref, k_ref, v_ref, *, group):
    outs = (q_ref, k_ref, v_ref)
    pairs = mine_ref.shape[1] // (3 * LANES)

    def put(source_ref, place):
        for p in range(pairs):
            at = (p // group) * 2 * group * LANES + place * group * LANES + (p % group) * LANES
            for i in range(3):
                start = (3 * p + i) * LANES
                outs[i][:, at : at + LANES] = source_ref[:, start : start + LANES].astype(f32)

    for place in range(2):

        @pl.when(place_ref[0] == place)
        def _():
            put(mine_ref, place)
            put(other_ref, 1 - place)


def spread_heads(place, mine, other, heads_width):
    rows, width = mine.shape
    full = 2 * width // 3
    block = min(rows, 128)
    return pl.pallas_call(
        functools.partial(spread_heads_kernel, group=heads_width // LANES),
        grid_spec=pltpu.PrefetchScalarGridSpec(
            num_scalar_prefetch=1,
            grid=(rows // block,),
            in_specs=[pl.BlockSpec((block, width), lambda i, p: (i, 0))] * 2,
            out_specs=[pl.BlockSpec((block, full), lambda i, p: (i, 0))] * 3,
        ),
        out_shape=[jax.ShapeDtypeStruct((rows, full), f32)] * 3,
        cost_estimate=pl.CostEstimate(
            flops=0, bytes_accessed=16 * rows * full, transcendentals=0
        ),
        name="spread_heads",
    )(place, mine, other)


def line_pairs(size, stride, first, last, step):
    return [
        (i * stride + o, (i + step) * stride + o)
        for i in range(first, last + 1)
        for o in range(stride)
    ]


def line_scatter(block_of, axis, size, stride=1):
    count = size // stride
    place = lax.axis_index(axis) // stride
    total = block_of(place).astype(f32)
    if count == 1:
        return total
    last = count - 1
    up, down = block_of(last), block_of(0)
    for s in range(last):
        up = lax.ppermute(up, axis, line_pairs(size, stride, 0, s, 1))
        down = lax.ppermute(down, axis, line_pairs(size, stride, last - s, last, -1))
        if s + 1 < last:
            here_up = block_of(jnp.minimum(last - 1 - s + place, last))
            here_down = block_of(jnp.maximum(place - (last - 1 - s), 0))
            up = (up.astype(f32) + here_up.astype(f32)).astype(bf16)
            down = (down.astype(f32) + here_down.astype(f32)).astype(bf16)
    return total + up.astype(f32) + down.astype(f32)


def line_gather(value, axis, size, stride=1):
    count = size // stride
    place = lax.axis_index(axis) // stride
    rows = value.shape[0]
    last = count - 1
    ups, downs = [value], [value]
    for s in range(last):
        ups.append(lax.ppermute(ups[-1], axis, line_pairs(size, stride, s, last - 1, 1)))
        downs.append(lax.ppermute(downs[-1], axis, line_pairs(size, stride, 1, last - s, -1)))
    out = jnp.zeros((count * rows,) + value.shape[1:], value.dtype)
    out = lax.dynamic_update_slice_in_dim(out, value, place * rows, 0)
    for s in range(last):
        came = lax.select_n(place - 1 - s >= 0, downs[last - s], ups[s + 1])
        out = lax.dynamic_update_slice_in_dim(
            out, came, lax.rem(place - 1 - s + count, count) * rows, 0
        )
    return out


def swap(value, axis, size, distance):
    return lax.ppermute(value, axis, [(i, i ^ distance) for i in range(size)])


def bit_orders(size):
    bits = [1 << b for b in range(size.bit_length() - 1)]
    return bits, bits[::-1]


def gather_rows(value, axis, size):
    half = value.shape[0] // 2
    parts = []
    for part, order in zip((value[:half], value[half:]), bit_orders(size)):
        held = {0: part}
        for bit in order:
            for d in list(held):
                held[d ^ bit] = swap(held[d], axis, size, bit)
        parts.append(held)
    return jnp.concatenate([parts[h][d] for d in range(size) for h in range(2)], axis=0)


def gather_in_order(value, place, axis, size):
    count = value.shape[0]
    half = count // 2
    out = jnp.zeros((size * count,) + value.shape[1:], value.dtype)
    for h, (part, order) in enumerate(zip((value[:half], value[half:]), bit_orders(size))):
        held = {0: part}
        for bit in order:
            for d in list(held):
                held[d ^ bit] = swap(held[d], axis, size, bit)
        for d, part in held.items():
            out = lax.dynamic_update_slice_in_dim(out, part, (place ^ d) * count + h * half, 0)
    return out


def scatter_rows(block_of, axis, size):
    blocks = {d: block_of(d) for d in range(size)}
    half = blocks[0].shape[0] // 2
    sums = []
    for h, order in enumerate(bit_orders(size)):
        held = {d: b[h * half : (h + 1) * half] for d, b in blocks.items()}
        for bit in order:
            for d in [d for d in held if d & bit]:
                came = swap(held.pop(d).astype(bf16), axis, size, bit)
                held[d ^ bit] = held[d ^ bit].astype(f32) + came.astype(f32)
        sums.append(held[0])
    return jnp.concatenate(sums, axis=0)


def local(
    tokens,
    cotangent,
    piece_start,
    attention_gain,
    query_weight,
    key_weight,
    value_weight,
    output_weight,
    feedforward_gain,
    gate_weight,
    up_weight,
    down_weight,
):
    lengths, shards, copies = (lax.axis_size(name) for name in ("seq", "fsdp", "rep"))
    batch, span, features = tokens.shape
    hidden = gate_weight.shape[1]
    team = lengths // batch
    members = lengths * copies
    everyone = ("seq", "rep")
    own_rows = batch * span
    length = lengths * span
    part = hidden // shards
    rows = features // shards
    heads_width = features // (shards * team)
    width = features // team
    z, f, r = (lax.axis_index(name) for name in ("seq", "fsdp", "rep"))
    line = z * copies + r
    mine = lax.rem(line, team)
    local_seq = lax.rem(line // team, batch)

    def perm_in(k):
        pairs = []
        for zz in range(lengths):
            for rr in range(copies):
                j = (zz + k) % batch
                pairs.append((zz * copies + rr, (rr * batch + j) * team + zz // batch))
        return pairs

    def take_sequence(value):
        came = [
            lax.ppermute(
                lax.dynamic_index_in_dim(value, lax.rem(z + k, batch), 0, False),
                everyone,
                perm_in(k),
            )
            for k in range(batch)
        ]
        return jnp.concatenate(
            [lax.select_n(lax.rem(local_seq + batch - b, batch), *came) for b in range(batch)],
            axis=0,
        )

    def give_back(value):
        blocks = value.reshape(batch, span, features)
        came = [
            lax.ppermute(
                lax.dynamic_index_in_dim(blocks, lax.rem(local_seq + batch - k, batch), 0, False),
                everyone,
                [(b, a) for a, b in perm_in(k)],
            )
            for k in range(batch)
        ]
        return jnp.stack(
            [lax.select_n(lax.rem(j + batch * lengths - z, batch), *came) for j in range(batch)]
        )

    def team_gather(value):
        came = [value] + [swap(value, everyone, members, d) for d in range(1, team)]
        return jnp.concatenate([lax.select_n(mine ^ u, *came) for u in range(team)], axis=0)

    def team_scatter(value):
        def block(d):
            return lax.dynamic_slice_in_dim(value, (mine ^ d) * own_rows, own_rows, 0)

        total = block(0).astype(f32)
        for d in range(1, team):
            total = total + swap(block(d), everyone, members, d).astype(f32)
        return total

    def shard_gather_small(value):
        out = jnp.zeros((shards,) + value.shape, value.dtype)
        for d in range(shards):
            came = swap(value, "fsdp", shards, d) if d else value
            out = lax.dynamic_update_index_in_dim(out, came, f ^ d, 0)
        return out

    def head_columns(weight):
        split = weight.reshape(weight.shape[0], shards, team, heads_width)
        return lax.dynamic_index_in_dim(split, mine, 2, False).reshape(weight.shape[0], width)

    tokens_own = take_sequence(tokens)
    start = lax.ppermute(
        lax.dynamic_index_in_dim(piece_start, lax.rem(z, batch), 0), everyone, perm_in(0)
    )

    pairs = width // LANES
    wqkv_rows = jnp.stack(
        [
            head_columns(w).reshape(rows, pairs, LANES)
            for w in (query_weight, key_weight, value_weight)
        ],
        axis=2,
    ).reshape(rows, 3 * width)
    wqkv = gather_in_order(wqkv_rows, f, "fsdp", shards)
    wo_rows = lax.dynamic_slice_in_dim(output_weight, mine * heads_width, heads_width, 0)
    wqkv, wo_rows, gate_weight, up_weight, cotangent = lax.optimization_barrier(
        (wqkv, wo_rows, gate_weight, up_weight, cotangent)
    )
    wo = gather_in_order(wo_rows, f, "fsdp", shards)

    gains = shard_gather_small(jnp.stack([attention_gain, feedforward_gain]))
    gain_first = gains[:, 0].reshape(features).astype(f32)
    gain_second = gains[:, 1].reshape(features).astype(f32)

    half_dim = HEAD_DIM // 2
    places = jnp.arange(length, dtype=jnp.int32).astype(f32)
    frequency = ROPE_BASE ** (-jnp.arange(half_dim, dtype=f32) / half_dim)
    angles = places[:, None] * frequency[None, :]
    cos_half, sin_half = jnp.cos(angles), jnp.sin(angles)
    cosine = jnp.concatenate([cos_half] * 4, axis=1)
    sine = jnp.concatenate([-sin_half, sin_half] * 2, axis=1)

    activation = tokens_own.astype(f32)
    scale_first = lax.rsqrt(jnp.mean(activation * activation, axis=-1, keepdims=True) + NORM_EPS)
    first_own = (activation * scale_first * gain_first).astype(bf16)
    first = team_gather(first_own)
    lin = matmul(first, wqkv)
    attended, qkv, lse = attend_forward(start, lin, cosine, sine)
    residual = activation + team_scatter(matmul(attended, wo, bf16))
    scale_second = lax.rsqrt(jnp.mean(residual * residual, axis=-1, keepdims=True) + NORM_EPS)
    second_own = (residual * scale_second * gain_second).astype(bf16)

    slab = part // copies

    def hidden_columns(weight):
        out = jnp.zeros((shards, rows, slab), bf16)
        for d in range(shards):
            piece = lax.dynamic_slice_in_dim(weight, (f ^ d) * part + r * slab, slab, 1)
            came = swap(piece, "fsdp", shards, d) if d else piece
            out = lax.dynamic_update_index_in_dim(out, came, f ^ d, 0)
        out = out.reshape(features, slab)
        came = [out] + [swap(out, "rep", copies, d) for d in range(1, copies)]
        return jnp.concatenate([lax.select_n(r ^ u, *came) for u in range(copies)], axis=1)

    gate_w = hidden_columns(gate_weight)
    up_w = hidden_columns(up_weight)

    cotangent_own = take_sequence(cotangent)
    cot = gather_rows(cotangent_own, "fsdp", shards)
    second = gather_rows(second_own, "fsdp", shards)

    gate = matmul(second, gate_w)
    up = matmul(second, up_w)
    inner_grad = against(cot, down_weight)
    sig = jax.nn.sigmoid(gate)
    silu = gate * sig
    inner = (silu * up).astype(bf16)
    gate_grad = (inner_grad * up * (sig * (1.0 + gate * (1.0 - sig)))).astype(bf16)
    up_grad = (inner_grad * silu).astype(bf16)

    second_grad_part = (against(gate_grad, gate_w) + against(up_grad, up_w)).astype(bf16)
    second_grad = scatter_rows(
        lambda d: second_grad_part[d * own_rows : (d + 1) * own_rows], "fsdp", shards
    )
    down_part = matmul(inner, down_weight, bf16)
    layer_rows = residual + scatter_rows(
        lambda d: down_part[d * own_rows : (d + 1) * own_rows], "fsdp", shards
    )
    layer_output = give_back(layer_rows.astype(bf16))

    def members_scatter(value):
        return lax.psum_scatter(value, everyone, scatter_dimension=0, tiled=True)

    def members_gather(value):
        return lax.all_gather(value, everyone, axis=0, tiled=False)

    down_piece = members_scatter(outer_sum(inner, cot, bf16))

    tiny = rows // members

    def member_major(term):
        blocks = term.reshape(shards, members, tiny, part)
        return blocks.transpose(1, 0, 2, 3).reshape(features, part)

    def shard_spread(piece):
        piece = piece.reshape(shards, tiny, part)
        out = jnp.zeros((tiny, hidden), bf16)
        for d in range(shards):
            came = lax.dynamic_index_in_dim(piece, f ^ d, 0, False)
            came = swap(came, "fsdp", shards, d) if d else came
            out = lax.dynamic_update_slice_in_dim(out, came, (f ^ d) * part, 1)
        return out

    gate_piece = members_scatter(member_major(outer_sum(second, gate_grad, bf16)))
    up_piece = members_scatter(member_major(outer_sum(second, up_grad, bf16)))
    down_grad = members_gather(down_piece).reshape(part, features).astype(f32)
    gate_grad_w = members_gather(shard_spread(gate_piece)).reshape(rows, hidden).astype(f32)
    up_grad_w = members_gather(shard_spread(up_piece)).reshape(rows, hidden).astype(f32)

    output_rows = cotangent_own.astype(f32)
    scaled = second_grad * gain_second
    residual_grad = (
        output_rows
        + scale_second * scaled
        - residual
        * (scale_second * scale_second * scale_second)
        * jnp.mean(scaled * residual, axis=-1, keepdims=True)
    )
    gain_second_term = jnp.sum(second_grad * residual * scale_second, axis=0)
    branch_own = residual_grad.astype(bf16)
    branch = team_gather(branch_own)

    attended_grad = against(branch, wo, bf16)
    wo_term = outer_sum(attended, branch, bf16)
    attended_grad, wo_term = lax.optimization_barrier((attended_grad, wo_term))
    lin_grad = attend_backward(start, qkv, attended, attended_grad, lse, cosine, sine)
    first_grad = team_scatter(against(lin_grad, wqkv, bf16))
    wqkv_term = outer_sum(first, lin_grad, bf16)

    scaled = first_grad * gain_first
    input_rows = (
        residual_grad
        + scale_first * scaled
        - activation
        * (scale_first * scale_first * scale_first)
        * jnp.mean(scaled * activation, axis=-1, keepdims=True)
    )
    gain_first_term = jnp.sum(first_grad * activation * scale_first, axis=0)
    input_gradient = give_back(input_rows.astype(bf16))

    def weight_rows(term):
        size = term.shape[0] // shards

        def block(d):
            return lax.dynamic_slice_in_dim(term, (f ^ d) * size, size, 0)

        return scatter_rows(block, "fsdp", shards).astype(bf16)

    stride = team // copies

    def line_sum(value):
        size = value.shape[0] * stride // lengths
        piece = line_scatter(
            lambda d: lax.dynamic_slice_in_dim(value, d * size, size, 0), "seq", lengths, stride
        )
        return line_gather(piece.astype(bf16), "seq", lengths, stride)

    wo_sum = line_sum(weight_rows(wo_term))
    wqkv_sum = line_sum(weight_rows(wqkv_term))

    def team_stack(value):
        came = [value] + [swap(value, everyone, members, d) for d in range(1, team)]
        return [lax.select_n(mine ^ u, *came) for u in range(team)]

    if team == 2 and heads_width % LANES == 0:
        place = mine.astype(jnp.int32).reshape(1)
        output_grad_w = widen_halves(place, wo_sum, swap(wo_sum, everyone, members, 1))
        head_gradients = spread_heads(
            place, wqkv_sum, swap(wqkv_sum, everyone, members, 1), heads_width
        )
    else:
        output_grad_w = jnp.concatenate(team_stack(wo_sum), axis=0).astype(f32)
        wqkv_all = [v.reshape(rows, pairs, 3, LANES) for v in team_stack(wqkv_sum)]

        def head_gradient(i):
            split = [v[:, :, i].reshape(rows, shards, heads_width) for v in wqkv_all]
            return jnp.stack(split, axis=2).reshape(rows, features).astype(f32)

        head_gradients = [head_gradient(i) for i in range(3)]

    gain_terms = jnp.stack([gain_first_term, gain_second_term])
    for axis, size in (("rep", copies), ("fsdp", shards), ("seq", lengths)):
        for bit in bit_orders(size)[0]:
            gain_terms = gain_terms + swap(gain_terms, axis, size, bit)
    gain_grads = lax.dynamic_slice_in_dim(gain_terms, f * rows, rows, 1)
    return (
        layer_output,
        input_gradient,
        gain_grads[0],
        head_gradients[0],
        head_gradients[1],
        head_gradients[2],
        output_grad_w,
        gain_grads[1],
        gate_grad_w,
        up_grad_w,
        down_grad,
    )


def solution(mesh):
    placed = (
        P(("fsdp", "rep"), "seq", None),
        P(("fsdp", "rep"), "seq", None),
        P(("fsdp", "rep")),
        P("fsdp"),
        P("fsdp", None),
        P("fsdp", None),
        P("fsdp", None),
        P("fsdp", None),
        P("fsdp"),
        P("fsdp", None),
        P("fsdp", None),
        P("fsdp", None),
    )
    return jax.shard_map(
        local,
        mesh=mesh,
        in_specs=placed,
        out_specs=(
            P(("fsdp", "rep"), "seq", None),
            P(("fsdp", "rep"), "seq", None),
            P("fsdp"),
            P("fsdp", None),
            P("fsdp", None),
            P("fsdp", None),
            P("fsdp", None),
            P("fsdp"),
            P("fsdp", None),
            P("fsdp", None),
            P("fsdp", None),
        ),
        check_vma=False,
    )
```

```python
import functools
import math

import jax
import jax.numpy as jnp
from jax import lax
from jax.experimental import pallas as pl
from jax.experimental.pallas import tpu as pltpu
from jax.sharding import PartitionSpec as P

HEADS = 32
HEAD_DIM = 64
PIECE = 256
BLOCK = 256
LANES = 128

NORM_EPS = 1e-05
ROPE_BASE = 130000.0
MASKED_SCORE = -1e30
SCALE = 0.125 * math.log2(math.e)

bf16 = jnp.bfloat16
f32 = jnp.float32


def matmul(left_op, right_op, out=f32):
    return jnp.dot(left_op, right_op, preferred_element_type=f32).astype(out)


def outer_sum(left_op, right_op, out=f32):
    return lax.dot_general(
        left_op, right_op, (((0,), (0,)), ((), ())), preferred_element_type=f32
    ).astype(out)


def against(left_op, right_op, out=f32):
    return lax.dot_general(
        left_op, right_op, (((1,), (1,)), ((), ())), preferred_element_type=f32
    ).astype(out)


def dot_nt(left_op, right_op):
    return lax.dot_general(
        left_op, right_op, (((1,), (1,)), ((), ())), preferred_element_type=f32
    )


def dot_nn(left_op, right_op):
    return lax.dot_general(
        left_op, right_op, (((1,), (0,)), ((), ())), preferred_element_type=f32
    )


def lane_index(rows):
    return lax.broadcasted_iota(jnp.int32, (rows, LANES), 1)


def turned(value, cosine, sine):
    front = lax.rem(lane_index(value.shape[0]), HEAD_DIM) < HEAD_DIM // 2
    swapped = jnp.where(
        front,
        pltpu.roll(value, LANES - HEAD_DIM // 2, 1),
        pltpu.roll(value, HEAD_DIM // 2, 1),
    )
    return value * cosine + swapped * sine


def per_head_rows(value):
    first = lane_index(value.shape[0]) < HEAD_DIM
    zero = jnp.zeros_like(value)
    return jnp.concatenate([jnp.where(first, value, zero), jnp.where(first, zero, value)], axis=0)


def from_head_columns(value):
    rows = value.shape[1] // 2
    first = lax.broadcasted_iota(jnp.int32, (LANES, rows), 0) < HEAD_DIM
    return jnp.where(first, value[:, :rows], value[:, rows:]).T


def seen(key_block, query_block, start):
    key_pos = key_block * BLOCK + lax.broadcasted_iota(jnp.int32, (BLOCK, 2 * BLOCK), 0)
    query_pos = query_block * BLOCK + lax.rem(
        lax.broadcasted_iota(jnp.int32, (BLOCK, 2 * BLOCK), 1), BLOCK
    )
    key_in = (key_pos >= start) & (key_pos < start + PIECE)
    query_in = (query_pos >= start) & (query_pos < start + PIECE)
    return (key_pos <= query_pos) | (key_in & query_in)


def spills_over(query_block, start):
    return (start > query_block * BLOCK) & (start < (query_block + 1) * BLOCK)


def attend_forward_kernel(
    start_ref, lin_ref, cos_ref, sin_ref, out_ref, qkv_ref, lse_ref, s_ref, m_ref, l_ref, acc_ref
):
    start = start_ref[0]
    blocks = lin_ref.shape[0] // BLOCK
    for i in range(blocks):
        rows = slice(i * BLOCK, (i + 1) * BLOCK)
        cosine, sine = cos_ref[rows, :], sin_ref[rows, :]
        for part in range(2):
            columns = slice(part * LANES, (part + 1) * LANES)
            qkv_ref[rows, columns] = turned(lin_ref[rows, columns], cosine, sine).astype(bf16)
        qkv_ref[rows, 2 * LANES :] = lin_ref[rows, 2 * LANES :].astype(bf16)

    def key_rows(j):
        return qkv_ref[j * BLOCK : (j + 1) * BLOCK, LANES : 2 * LANES]

    def value_columns(j):
        return qkv_ref[j * BLOCK : (j + 1) * BLOCK, 2 * LANES :].T

    for i in range(blocks):
        rows = slice(i * BLOCK, (i + 1) * BLOCK)
        queries = per_head_rows(qkv_ref[rows, :LANES])
        over = spills_over(i, start)
        top = None
        for j in range(i + 1):
            scores = dot_nt(key_rows(j), queries)
            if j == i:
                scores = jnp.where(seen(j, i, start), scores, MASKED_SCORE)
            s_ref[j * BLOCK : (j + 1) * BLOCK, :] = scores
            best = jnp.max(scores, axis=0, keepdims=True)
            top = best if top is None else jnp.maximum(top, best)
        m_ref[...] = top

        if i + 1 < blocks:

            @pl.when(over)
            def _():
                scores = dot_nt(key_rows(i + 1), queries)
                scores = jnp.where(seen(i + 1, i, start), scores, MASKED_SCORE)
                s_ref[(i + 1) * BLOCK : (i + 2) * BLOCK, :] = scores
                m_ref[...] = jnp.maximum(m_ref[...], jnp.max(scores, axis=0, keepdims=True))

        top = m_ref[...]
        shift = top * SCALE
        total, mixed = None, None
        for j in range(i + 1):
            weights = jnp.exp2(s_ref[j * BLOCK : (j + 1) * BLOCK, :] * SCALE - shift)
            part_total = jnp.sum(weights, axis=0, keepdims=True)
            part_mixed = dot_nn(value_columns(j), weights.astype(bf16))
            total = part_total if total is None else total + part_total
            mixed = part_mixed if mixed is None else mixed + part_mixed
        l_ref[...] = total
        acc_ref[...] = mixed

        if i + 1 < blocks:

            @pl.when(over)
            def _():
                weights = jnp.exp2(s_ref[(i + 1) * BLOCK : (i + 2) * BLOCK, :] * SCALE - shift)
                l_ref[...] += jnp.sum(weights, axis=0, keepdims=True)
                acc_ref[...] += dot_nn(value_columns(i + 1), weights.astype(bf16))

        total = l_ref[...]
        out_ref[rows, :] = from_head_columns(acc_ref[...] / total).astype(bf16)
        lse_ref[0, i : i + 1, :] = shift + jnp.log2(total)


def attend_backward_kernel(
    start_ref, qkv_ref, out_ref, grad_ref, lse_ref, cos_ref, sin_ref, lin_ref, dq_ref, dk_ref, dv_ref
):
    start = start_ref[0]
    blocks = qkv_ref.shape[0] // BLOCK
    dk_ref[...] = jnp.zeros_like(dk_ref)
    dv_ref[...] = jnp.zeros_like(dv_ref)
    for i in range(blocks):
        rows = slice(i * BLOCK, (i + 1) * BLOCK)
        queries = per_head_rows(qkv_ref[rows, :LANES])
        grads_in = grad_ref[rows, :]
        grads = per_head_rows(grads_in)
        both = (grads_in.astype(f32) * out_ref[rows, :].astype(f32)).T
        delta = jnp.concatenate(
            [
                jnp.sum(both[:HEAD_DIM], axis=0, keepdims=True),
                jnp.sum(both[HEAD_DIM:], axis=0, keepdims=True),
            ],
            axis=1,
        )
        lse = lse_ref[0, i : i + 1, :]

        def one(j, masked):
            keys_at = slice(j * BLOCK, (j + 1) * BLOCK)
            keys = qkv_ref[keys_at, LANES : 2 * LANES]
            scores = dot_nt(keys, queries)
            weights = jnp.exp2(scores * SCALE - lse)
            if masked:
                weights = jnp.where(seen(j, i, start), weights, 0.0)
            weight_grads = dot_nt(qkv_ref[keys_at, 2 * LANES :], grads)
            score_grads = (weights * (weight_grads - delta)).astype(bf16)
            dv_ref[keys_at, :] += dot_nn(weights.astype(bf16), grads)
            dk_ref[keys_at, :] += dot_nn(score_grads, queries)
            return dot_nn(keys.T, score_grads)

        query_grads = None
        for j in range(i + 1):
            part = one(j, j == i)
            query_grads = part if query_grads is None else query_grads + part
        dq_ref[...] = query_grads

        if i + 1 < blocks:

            @pl.when(spills_over(i, start))
            def _():
                dq_ref[...] += one(i + 1, True)

        lin_ref[rows, :LANES] = turned(
            from_head_columns(dq_ref[...]) * 0.125, cos_ref[rows, :], -sin_ref[rows, :]
        ).astype(bf16)
    for i in range(blocks):
        rows = slice(i * BLOCK, (i + 1) * BLOCK)
        lin_ref[rows, LANES : 2 * LANES] = turned(
            dk_ref[rows, :] * 0.125, cos_ref[rows, :], -sin_ref[rows, :]
        ).astype(bf16)
        lin_ref[rows, 2 * LANES :] = dv_ref[rows, :].astype(bf16)


def column_block(length, width):
    return pl.BlockSpec((length, width), lambda p, s: (0, p))


def whole_block(shape):
    return pl.BlockSpec(shape, lambda p, s: (0,) * len(shape))


def attend_forward(start, lin, cosine, sine):
    length, width = lin.shape
    pairs = width // (3 * LANES)
    blocks = length // BLOCK
    flops = pairs * 2 * 2 * 2 * length * length * LANES
    return pl.pallas_call(
        attend_forward_kernel,
        grid_spec=pltpu.PrefetchScalarGridSpec(
            num_scalar_prefetch=1,
            grid=(pairs,),
            in_specs=[
                column_block(length, 3 * LANES),
                whole_block((length, LANES)),
                whole_block((length, LANES)),
            ],
            out_specs=[
                column_block(length, LANES),
                column_block(length, 3 * LANES),
                pl.BlockSpec((1, blocks, 2 * BLOCK), lambda p, s: (p, 0, 0)),
            ],
            scratch_shapes=[
                pltpu.VMEM((length, 2 * BLOCK), f32),
                pltpu.VMEM((1, 2 * BLOCK), f32),
                pltpu.VMEM((1, 2 * BLOCK), f32),
                pltpu.VMEM((LANES, 2 * BLOCK), f32),
            ],
        ),
        out_shape=[
            jax.ShapeDtypeStruct((length, pairs * LANES), bf16),
            jax.ShapeDtypeStruct((length, width), bf16),
            jax.ShapeDtypeStruct((pairs, blocks, 2 * BLOCK), f32),
        ],
        cost_estimate=pl.CostEstimate(
            flops=flops,
            bytes_accessed=length * width * 6 + length * pairs * LANES * 2,
            transcendentals=pairs * 2 * length * length // 2,
        ),
        name="attend_forward",
    )(start, lin, cosine, sine)


def attend_backward(start, qkv, out, grad, lse, cosine, sine):
    length, width = qkv.shape
    pairs = width // (3 * LANES)
    blocks = length // BLOCK
    flops = pairs * 2 * 5 * 2 * length * length * LANES
    return pl.pallas_call(
        attend_backward_kernel,
        grid_spec=pltpu.PrefetchScalarGridSpec(
            num_scalar_prefetch=1,
            grid=(pairs,),
            in_specs=[
                column_block(length, 3 * LANES),
                column_block(length, LANES),
                column_block(length, LANES),
                pl.BlockSpec((1, blocks, 2 * BLOCK), lambda p, s: (p, 0, 0)),
                whole_block((length, LANES)),
                whole_block((length, LANES)),
            ],
            out_specs=column_block(length, 3 * LANES),
            scratch_shapes=[
                pltpu.VMEM((LANES, 2 * BLOCK), f32),
                pltpu.VMEM((length, LANES), f32),
                pltpu.VMEM((length, LANES), f32),
            ],
        ),
        out_shape=jax.ShapeDtypeStruct((length, width), bf16),
        cost_estimate=pl.CostEstimate(
            flops=flops,
            bytes_accessed=length * width * 4 + length * pairs * LANES * 4,
            transcendentals=pairs * 2 * length * length // 2,
        ),
        name="attend_backward",
    )(start, qkv, out, grad, lse, cosine, sine)


def widen_kernel(place_ref, mine_ref, other_ref, out_ref):
    own = pl.program_id(0) == place_ref[0]

    @pl.when(own)
    def _():
        out_ref[...] = mine_ref[...].astype(f32)

    @pl.when(jnp.logical_not(own))
    def _():
        out_ref[...] = other_ref[...].astype(f32)


def widen_halves(place, mine, other):
    rows, width = mine.shape
    block = rows
    while block * width > 512 * 1024 and block % 32 == 0:
        block //= 2
    steps = rows // block
    return pl.pallas_call(
        widen_kernel,
        grid_spec=pltpu.PrefetchScalarGridSpec(
            num_scalar_prefetch=1,
            grid=(2, steps),
            in_specs=[
                pl.BlockSpec((block, width), lambda u, i, p: (jnp.where(u == p[0], i, 0), 0)),
                pl.BlockSpec((block, width), lambda u, i, p: (jnp.where(u == p[0], 0, i), 0)),
            ],
            out_specs=pl.BlockSpec((block, width), lambda u, i, p: (u * steps + i, 0)),
        ),
        out_shape=jax.ShapeDtypeStruct((2 * rows, width), f32),
        cost_estimate=pl.CostEstimate(
            flops=0, bytes_accessed=12 * rows * width, transcendentals=0
        ),
        name="widen_halves",
    )(place, mine, other)


def pick_heads_kernel(place_ref, q_ref, k_ref, v_ref, out_ref):
    for p in range(q_ref.shape[1] // LANES):
        for i, part_ref in enumerate((q_ref, k_ref, v_ref)):
            at = (3 * p + i) * LANES
            out_ref[:, at : at + LANES] = part_ref[:, p * LANES : (p + 1) * LANES]


def pick_heads(place, weights, heads_width, team):
    rows, full = weights[0].shape
    groups = full // (heads_width * team)
    return pl.pallas_call(
        pick_heads_kernel,
        grid_spec=pltpu.PrefetchScalarGridSpec(
            num_scalar_prefetch=1,
            grid=(groups,),
            in_specs=[pl.BlockSpec((rows, heads_width), lambda s, p: (0, s * team + p[0]))] * 3,
            out_specs=pl.BlockSpec((rows, 3 * heads_width), lambda s, p: (0, s)),
        ),
        out_shape=jax.ShapeDtypeStruct((rows, 3 * full // team), bf16),
        cost_estimate=pl.CostEstimate(
            flops=0, bytes_accessed=12 * rows * full // team, transcendentals=0
        ),
        name="pick_heads",
    )(place, *weights)


def spread_heads_kernel(place_ref, mine_ref, other_ref, q_ref, k_ref, v_ref, *, group):
    outs = (q_ref, k_ref, v_ref)
    pairs = mine_ref.shape[1] // (3 * LANES)

    def put(source_ref, place):
        for p in range(pairs):
            at = (p // group) * 2 * group * LANES + place * group * LANES + (p % group) * LANES
            for i in range(3):
                start = (3 * p + i) * LANES
                outs[i][:, at : at + LANES] = source_ref[:, start : start + LANES].astype(f32)

    for place in range(2):

        @pl.when(place_ref[0] == place)
        def _():
            put(mine_ref, place)
            put(other_ref, 1 - place)


def spread_heads(place, mine, other, heads_width):
    rows, width = mine.shape
    full = 2 * width // 3
    block = min(rows, 128)
    return pl.pallas_call(
        functools.partial(spread_heads_kernel, group=heads_width // LANES),
        grid_spec=pltpu.PrefetchScalarGridSpec(
            num_scalar_prefetch=1,
            grid=(rows // block,),
            in_specs=[pl.BlockSpec((block, width), lambda i, p: (i, 0))] * 2,
            out_specs=[pl.BlockSpec((block, full), lambda i, p: (i, 0))] * 3,
        ),
        out_shape=[jax.ShapeDtypeStruct((rows, full), f32)] * 3,
        cost_estimate=pl.CostEstimate(
            flops=0, bytes_accessed=16 * rows * full, transcendentals=0
        ),
        name="spread_heads",
    )(place, mine, other)


def line_pairs(size, stride, first, last, step):
    return [
        (i * stride + o, (i + step) * stride + o)
        for i in range(first, last + 1)
        for o in range(stride)
    ]


def line_scatter(block_of, axis, size, stride=1):
    count = size // stride
    place = lax.axis_index(axis) // stride
    total = block_of(place).astype(f32)
    if count == 1:
        return total
    last = count - 1
    up, down = block_of(last), block_of(0)
    for s in range(last):
        up = lax.ppermute(up, axis, line_pairs(size, stride, 0, s, 1))
        down = lax.ppermute(down, axis, line_pairs(size, stride, last - s, last, -1))
        if s + 1 < last:
            here_up = block_of(jnp.minimum(last - 1 - s + place, last))
            here_down = block_of(jnp.maximum(place - (last - 1 - s), 0))
            up = (up.astype(f32) + here_up.astype(f32)).astype(bf16)
            down = (down.astype(f32) + here_down.astype(f32)).astype(bf16)
    return total + up.astype(f32) + down.astype(f32)


def line_gather(value, axis, size, stride=1):
    count = size // stride
    place = lax.axis_index(axis) // stride
    rows = value.shape[0]
    last = count - 1
    ups, downs = [value], [value]
    for s in range(last):
        ups.append(lax.ppermute(ups[-1], axis, line_pairs(size, stride, s, last - 1, 1)))
        downs.append(lax.ppermute(downs[-1], axis, line_pairs(size, stride, 1, last - s, -1)))
    out = jnp.zeros((count * rows,) + value.shape[1:], value.dtype)
    out = lax.dynamic_update_slice_in_dim(out, value, place * rows, 0)
    for s in range(last):
        came = lax.select_n(place - 1 - s >= 0, downs[last - s], ups[s + 1])
        out = lax.dynamic_update_slice_in_dim(
            out, came, lax.rem(place - 1 - s + count, count) * rows, 0
        )
    return out


def together(*values):
    return lax.optimization_barrier(values)


def swap(value, axis, size, distance):
    return lax.ppermute(value, axis, [(i, i ^ distance) for i in range(size)])


def bit_orders(size):
    bits = [1 << b for b in range(size.bit_length() - 1)]
    return bits, bits[::-1]


def xor_places(order):
    places = [0]
    for bit in order:
        places += [d ^ bit for d in places]
    return places


def gather_in_order(value, place, axis, size):
    count = value.shape[0]
    half = count // 2
    out = jnp.zeros((size * count,) + value.shape[1:], value.dtype)
    for h, order in enumerate(bit_orders(size)):
        held = value[h * half : (h + 1) * half]
        for bit in order:
            held = jnp.concatenate([held, swap(held, axis, size, bit)], axis=0)
        for i, d in enumerate(xor_places(order)):
            out = lax.dynamic_update_slice_in_dim(
                out, held[i * half : (i + 1) * half], (place ^ d) * count + h * half, 0
            )
    return out


def scatter_in_order(value, place, axis, size):
    count = value.shape[0] // size
    half = count // 2
    sums = []
    for h, order in enumerate(bit_orders(size)):
        blocks = [
            lax.dynamic_slice_in_dim(value, (place ^ d) * count + h * half, half, 0)
            for d in xor_places(order)
        ]
        kept = len(blocks) // 2
        sent = jnp.concatenate(blocks[kept:], axis=0)
        total = jnp.concatenate(blocks[:kept], axis=0).astype(f32)
        for step, bit in enumerate(order[::-1]):
            if step:
                middle = total.shape[0] // 2
                sent, total = total[middle:].astype(bf16), total[:middle]
            total = total + swap(sent, axis, size, bit).astype(f32)
        sums.append(total)
    return jnp.concatenate(sums, axis=0)


def local(
    tokens,
    cotangent,
    piece_start,
    attention_gain,
    query_weight,
    key_weight,
    value_weight,
    output_weight,
    feedforward_gain,
    gate_weight,
    up_weight,
    down_weight,
):
    lengths, shards, copies = (lax.axis_size(name) for name in ("seq", "fsdp", "rep"))
    batch, span, features = tokens.shape
    hidden = gate_weight.shape[1]
    team = lengths // batch
    members = lengths * copies
    everyone = ("seq", "rep")
    own_rows = batch * span
    length = lengths * span
    part = hidden // shards
    rows = features // shards
    heads_width = features // (shards * team)
    width = features // team
    z, f, r = (lax.axis_index(name) for name in ("seq", "fsdp", "rep"))
    line = z * copies + r
    mine = lax.rem(line, team)
    local_seq = lax.rem(line // team, batch)

    def perm_in(k):
        pairs = []
        for zz in range(lengths):
            for rr in range(copies):
                j = (zz + k) % batch
                pairs.append((zz * copies + rr, (rr * batch + j) * team + zz // batch))
        return pairs

    def take_sequence(value):
        came = [
            lax.ppermute(
                lax.dynamic_index_in_dim(value, lax.rem(z + k, batch), 0, False),
                everyone,
                perm_in(k),
            )
            for k in range(batch)
        ]
        return jnp.concatenate(
            [lax.select_n(lax.rem(local_seq + batch - b, batch), *came) for b in range(batch)],
            axis=0,
        )

    def give_back(value):
        blocks = value.reshape(batch, span, features)
        came = [
            lax.ppermute(
                lax.dynamic_index_in_dim(blocks, lax.rem(local_seq + batch - k, batch), 0, False),
                everyone,
                [(b, a) for a, b in perm_in(k)],
            )
            for k in range(batch)
        ]
        return jnp.stack(
            [lax.select_n(lax.rem(j + batch * lengths - z, batch), *came) for j in range(batch)]
        )

    def team_gather(value):
        came = [value] + [swap(value, everyone, members, d) for d in range(1, team)]
        return jnp.concatenate([lax.select_n(mine ^ u, *came) for u in range(team)], axis=0)

    def team_scatter(value):
        def block(d):
            return lax.dynamic_slice_in_dim(value, (mine ^ d) * own_rows, own_rows, 0)

        total = block(0).astype(f32)
        for d in range(1, team):
            total = total + swap(block(d), everyone, members, d).astype(f32)
        return total

    def shard_gather_small(value):
        out = jnp.zeros((shards,) + value.shape, value.dtype)
        for d in range(shards):
            came = swap(value, "fsdp", shards, d) if d else value
            out = lax.dynamic_update_index_in_dim(out, came, f ^ d, 0)
        return out

    def head_columns(weight):
        split = weight.reshape(weight.shape[0], shards, team, heads_width)
        return lax.dynamic_index_in_dim(split, mine, 2, False).reshape(weight.shape[0], width)

    tokens_own = take_sequence(tokens)
    start = lax.ppermute(
        lax.dynamic_index_in_dim(piece_start, lax.rem(z, batch), 0), everyone, perm_in(0)
    )

    pairs = width // LANES
    if heads_width % LANES == 0:
        wqkv_rows = pick_heads(
            mine.astype(jnp.int32).reshape(1),
            (query_weight, key_weight, value_weight),
            heads_width,
            team,
        )
    else:
        wqkv_rows = jnp.stack(
            [
                head_columns(w).reshape(rows, pairs, LANES)
                for w in (query_weight, key_weight, value_weight)
            ],
            axis=2,
        ).reshape(rows, 3 * width)
    wqkv = gather_in_order(wqkv_rows, f, "fsdp", shards)
    wo_rows = lax.dynamic_slice_in_dim(output_weight, mine * heads_width, heads_width, 0)
    cotangent_own = take_sequence(cotangent)
    wqkv, wo_rows, gate_weight, up_weight, cotangent_own = together(
        wqkv, wo_rows, gate_weight, up_weight, cotangent_own
    )
    wo = lax.all_gather(wo_rows, "fsdp", axis=0, tiled=True)
    wo, cotangent_own = together(wo, cotangent_own)
    cot = lax.all_gather(cotangent_own, "fsdp", axis=0, tiled=True)

    slab = part // copies

    split = rows // 2
    z_low = lax.rem(z, 2)

    def column_pieces(weight, d, row):
        return lax.dynamic_slice(weight, (row, (f ^ d) * part + r * slab), (split, slab))

    fetched = [
        swap(
            jnp.stack([column_pieces(w, d, z_low * split) for w in (gate_weight, up_weight)]),
            "fsdp",
            shards,
            d,
        )
        for d in range(1, shards)
    ]

    def join_columns(i, weight, halves):
        out = jnp.zeros((shards, rows, slab), bf16)
        own = lax.dynamic_slice_in_dim(weight, f * part + r * slab, slab, 1)
        out = lax.dynamic_update_index_in_dim(out, own, f, 0)
        for low in range(2):
            for d in range(1, shards):
                piece = lax.select_n(z_low == low, halves[1][d - 1, i], halves[0][d - 1, i])
                out = lax.dynamic_update_slice(out, piece[None], (f ^ d, low * split, 0))
        out = out.reshape(features, slab)
        came = [out] + [swap(out, "rep", copies, d) for d in range(1, copies)]
        return jnp.concatenate([lax.select_n(r ^ u, *came) for u in range(copies)], axis=1)

    gains = shard_gather_small(jnp.stack([attention_gain, feedforward_gain]))
    gain_first = gains[:, 0].reshape(features).astype(f32)
    gain_second = gains[:, 1].reshape(features).astype(f32)

    half_dim = HEAD_DIM // 2
    places = jnp.arange(length, dtype=jnp.int32).astype(f32)
    frequency = ROPE_BASE ** (-jnp.arange(half_dim, dtype=f32) / half_dim)
    angles = places[:, None] * frequency[None, :]
    cos_half, sin_half = jnp.cos(angles), jnp.sin(angles)
    cosine = jnp.concatenate([cos_half] * 4, axis=1)
    sine = jnp.concatenate([-sin_half, sin_half] * 2, axis=1)

    activation = tokens_own.astype(f32)
    scale_first = lax.rsqrt(jnp.mean(activation * activation, axis=-1, keepdims=True) + NORM_EPS)
    first_own = (activation * scale_first * gain_first).astype(bf16)
    first = team_gather(first_own)
    lin = matmul(first, wqkv)
    attended, qkv, lse = attend_forward(start, lin, cosine, sine)
    attended, *fetched = together(attended, *fetched)
    fetched = jnp.stack(fetched)
    exchanged = swap(fetched, "seq", lengths, 1)
    residual = activation + team_scatter(matmul(attended, wo, bf16))
    scale_second = lax.rsqrt(jnp.mean(residual * residual, axis=-1, keepdims=True) + NORM_EPS)
    second_own = (residual * scale_second * gain_second).astype(bf16)

    gate_w = join_columns(0, gate_weight, (fetched, exchanged))
    up_w = join_columns(1, up_weight, (fetched, exchanged))
    second = gather_in_order(second_own, f, "fsdp", shards)

    inner_grad = against(cot, down_weight)
    second, inner_grad = together(second, inner_grad)
    gate = matmul(second, gate_w)
    up = matmul(second, up_w)
    sig = jax.nn.sigmoid(gate)
    silu = gate * sig
    inner = (silu * up).astype(bf16)
    gate_grad = (inner_grad * up * (sig * (1.0 + gate * (1.0 - sig)))).astype(bf16)
    up_grad = (inner_grad * silu).astype(bf16)

    tiny = rows // members

    def member_major(term):
        blocks = term.reshape(shards, members, tiny, part)
        return blocks.transpose(1, 0, 2, 3).reshape(features, part)

    down_term = outer_sum(inner, cot, bf16)
    gate_grad, up_grad, down_term = together(gate_grad, up_grad, down_term)
    second_grad_part = (against(gate_grad, gate_w) + against(up_grad, up_w)).astype(bf16)
    second_grad_part, gate_grad, up_grad, inner = together(
        second_grad_part, gate_grad, up_grad, inner
    )
    gate_term = member_major(outer_sum(second, gate_grad, bf16))
    up_term = member_major(outer_sum(second, up_grad, bf16))
    down_part = matmul(inner, down_weight, bf16)
    second_grad = scatter_in_order(second_grad_part, f, "fsdp", shards)

    def members_scatter(value):
        return lax.psum_scatter(value, everyone, scatter_dimension=0, tiled=True)

    def members_gather(value):
        return lax.all_gather(value, everyone, axis=0, tiled=False)

    gate_piece = members_scatter(gate_term)
    up_piece = members_scatter(up_term)
    down_piece = members_scatter(down_term)

    def shard_spread(piece):
        piece = piece.reshape(shards, tiny, part)
        out = jnp.zeros((tiny, hidden), bf16)
        for d in range(shards):
            came = lax.dynamic_index_in_dim(piece, f ^ d, 0, False)
            came = swap(came, "fsdp", shards, d) if d else came
            out = lax.dynamic_update_slice_in_dim(out, came, (f ^ d) * part, 1)
        return out

    gate_spread = shard_spread(gate_piece)
    up_spread = shard_spread(up_piece)

    output_rows = cotangent_own.astype(f32)
    scaled = second_grad * gain_second
    residual_grad = (
        output_rows
        + scale_second * scaled
        - residual
        * (scale_second * scale_second * scale_second)
        * jnp.mean(scaled * residual, axis=-1, keepdims=True)
    )
    gain_second_term = jnp.sum(second_grad * residual * scale_second, axis=0)
    branch_own = residual_grad.astype(bf16)
    branch_own, down_part = together(branch_own, down_part)
    layer_rows = residual + scatter_in_order(down_part, f, "fsdp", shards)
    branch = team_gather(branch_own)

    attended_grad = against(branch, wo, bf16)
    wo_term = outer_sum(attended, branch, bf16)
    attended_grad, wo_term = together(attended_grad, wo_term)
    wo_own = scatter_in_order(wo_term, f, "fsdp", shards).astype(bf16)
    lin_grad = attend_backward(start, qkv, attended, attended_grad, lse, cosine, sine)
    lin_grad, gate_spread = together(lin_grad, gate_spread)
    wqkv_term = outer_sum(first, lin_grad, bf16)
    wqkv_term, up_spread, wo_own, layer_rows = together(
        wqkv_term, up_spread, wo_own, layer_rows
    )
    layer_output = give_back(layer_rows.astype(bf16))
    wqkv_own = scatter_in_order(wqkv_term, f, "fsdp", shards).astype(bf16)
    wqkv_own, first_grad, layer_output = together(
        wqkv_own, team_scatter(against(lin_grad, wqkv, bf16)), layer_output
    )
    down_grad = members_gather(down_piece).reshape(part, features).astype(f32)
    gate_grad_w = members_gather(gate_spread).reshape(rows, hidden).astype(f32)
    up_grad_w = members_gather(up_spread).reshape(rows, hidden).astype(f32)

    scaled = first_grad * gain_first
    input_rows = (
        residual_grad
        + scale_first * scaled
        - activation
        * (scale_first * scale_first * scale_first)
        * jnp.mean(scaled * activation, axis=-1, keepdims=True)
    )
    gain_first_term = jnp.sum(first_grad * activation * scale_first, axis=0)
    input_gradient = give_back(input_rows.astype(bf16))

    stride = team // copies
    line = lengths // stride
    wo_rows = heads_width // line

    wo_own = wo_own.reshape(line, wo_rows, features)
    wo_own = jnp.concatenate([wo_own[:, :, t * width : (t + 1) * width] for t in range(team)], 1)
    packed = jnp.concatenate([wqkv_own, wo_own.reshape(rows, width)], axis=1)
    size = rows // line
    packed = line_scatter(
        lambda d: lax.dynamic_slice_in_dim(packed, d * size, size, 0), "seq", lengths, stride
    )
    gain_terms = jnp.stack([gain_first_term, gain_second_term])
    for axis, size in (("rep", copies), ("fsdp", shards), ("seq", lengths)):
        for bit in bit_orders(size)[0]:
            gain_terms = gain_terms + swap(gain_terms, axis, size, bit)
    packed, gain_terms = together(packed.astype(bf16), gain_terms)
    packed = line_gather(packed, "seq", lengths, stride)

    def unpack(value):
        out = value[:, 3 * width :].reshape(line, team, wo_rows, width)
        out = jnp.concatenate([out[:, t] for t in range(team)], axis=2)
        return value[:, : 3 * width], out.reshape(heads_width, features)

    def team_stack(value):
        came = [value] + [swap(value, everyone, members, d) for d in range(1, team)]
        return [lax.select_n(mine ^ u, *came) for u in range(team)]

    if team == 2 and heads_width % LANES == 0:
        place = mine.astype(jnp.int32).reshape(1)
        wqkv_sum, wo_sum = unpack(packed)
        wqkv_other, wo_other = unpack(swap(packed, everyone, members, 1))
        output_grad_w = widen_halves(place, wo_sum, wo_other)
        head_gradients = spread_heads(place, wqkv_sum, wqkv_other, heads_width)
    else:
        sums = [unpack(v) for v in team_stack(packed)]
        output_grad_w = jnp.concatenate([v for _, v in sums], axis=0).astype(f32)
        wqkv_all = [v.reshape(rows, pairs, 3, LANES) for v, _ in sums]

        def head_gradient(i):
            split = [v[:, :, i].reshape(rows, shards, heads_width) for v in wqkv_all]
            return jnp.stack(split, axis=2).reshape(rows, features).astype(f32)

        head_gradients = [head_gradient(i) for i in range(3)]

    gain_grads = lax.dynamic_slice_in_dim(gain_terms, f * rows, rows, 1)
    return (
        layer_output,
        input_gradient,
        gain_grads[0],
        head_gradients[0],
        head_gradients[1],
        head_gradients[2],
        output_grad_w,
        gain_grads[1],
        gate_grad_w,
        up_grad_w,
        down_grad,
    )


def solution(mesh):
    placed = (
        P(("fsdp", "rep"), "seq", None),
        P(("fsdp", "rep"), "seq", None),
        P(("fsdp", "rep")),
        P("fsdp"),
        P("fsdp", None),
        P("fsdp", None),
        P("fsdp", None),
        P("fsdp", None),
        P("fsdp"),
        P("fsdp", None),
        P("fsdp", None),
        P("fsdp", None),
    )
    return jax.shard_map(
        local,
        mesh=mesh,
        in_specs=placed,
        out_specs=(
            P(("fsdp", "rep"), "seq", None),
            P(("fsdp", "rep"), "seq", None),
            P("fsdp"),
            P("fsdp", None),
            P("fsdp", None),
            P("fsdp", None),
            P("fsdp", None),
            P("fsdp"),
            P("fsdp", None),
            P("fsdp", None),
            P("fsdp", None),
        ),
        check_vma=False,
    )
```

```python
import functools
import math

import jax
import jax.numpy as jnp
from jax import lax
from jax.experimental import pallas as pl
from jax.experimental.pallas import tpu as pltpu
from jax.sharding import PartitionSpec as P

HEADS = 32
HEAD_DIM = 64
PIECE = 256
BLOCK = 256
LANES = 128

NORM_EPS = 1e-05
ROPE_BASE = 130000.0
MASKED_SCORE = -1e30
SCALE = 0.125 * math.log2(math.e)

bf16 = jnp.bfloat16
f32 = jnp.float32


def matmul(left_op, right_op, out=f32):
    return jnp.dot(left_op, right_op, preferred_element_type=f32).astype(out)


def outer_sum(left_op, right_op, out=f32):
    return lax.dot_general(
        left_op, right_op, (((0,), (0,)), ((), ())), preferred_element_type=f32
    ).astype(out)


def against(left_op, right_op, out=f32):
    return lax.dot_general(
        left_op, right_op, (((1,), (1,)), ((), ())), preferred_element_type=f32
    ).astype(out)


def dot_nt(left_op, right_op):
    return lax.dot_general(
        left_op, right_op, (((1,), (1,)), ((), ())), preferred_element_type=f32
    )


def dot_nn(left_op, right_op):
    return lax.dot_general(
        left_op, right_op, (((1,), (0,)), ((), ())), preferred_element_type=f32
    )


def lane_index(rows):
    return lax.broadcasted_iota(jnp.int32, (rows, LANES), 1)


def turned(value, cosine, sine):
    front = lax.rem(lane_index(value.shape[0]), HEAD_DIM) < HEAD_DIM // 2
    swapped = jnp.where(
        front,
        pltpu.roll(value, LANES - HEAD_DIM // 2, 1),
        pltpu.roll(value, HEAD_DIM // 2, 1),
    )
    return value * cosine + swapped * sine


def per_head_rows(value):
    first = lane_index(value.shape[0]) < HEAD_DIM
    zero = jnp.zeros_like(value)
    return jnp.concatenate([jnp.where(first, value, zero), jnp.where(first, zero, value)], axis=0)


def from_head_columns(value):
    rows = value.shape[1] // 2
    first = lax.broadcasted_iota(jnp.int32, (LANES, rows), 0) < HEAD_DIM
    return jnp.where(first, value[:, :rows], value[:, rows:]).T


def seen(key_block, query_block, start):
    key_pos = key_block * BLOCK + lax.broadcasted_iota(jnp.int32, (BLOCK, 2 * BLOCK), 0)
    query_pos = query_block * BLOCK + lax.rem(
        lax.broadcasted_iota(jnp.int32, (BLOCK, 2 * BLOCK), 1), BLOCK
    )
    key_in = (key_pos >= start) & (key_pos < start + PIECE)
    query_in = (query_pos >= start) & (query_pos < start + PIECE)
    return (key_pos <= query_pos) | (key_in & query_in)


def spills_over(query_block, start):
    return (start > query_block * BLOCK) & (start < (query_block + 1) * BLOCK)


def attend_forward_kernel(
    start_ref, lin_ref, cos_ref, sin_ref, out_ref, qkv_ref, lse_ref, s_ref, m_ref, l_ref, acc_ref
):
    start = start_ref[0]
    blocks = lin_ref.shape[0] // BLOCK
    for i in range(blocks):
        rows = slice(i * BLOCK, (i + 1) * BLOCK)
        cosine, sine = cos_ref[rows, :], sin_ref[rows, :]
        for part in range(2):
            columns = slice(part * LANES, (part + 1) * LANES)
            qkv_ref[rows, columns] = turned(lin_ref[rows, columns], cosine, sine).astype(bf16)
        qkv_ref[rows, 2 * LANES :] = lin_ref[rows, 2 * LANES :].astype(bf16)

    def key_rows(j):
        return qkv_ref[j * BLOCK : (j + 1) * BLOCK, LANES : 2 * LANES]

    def value_columns(j):
        return qkv_ref[j * BLOCK : (j + 1) * BLOCK, 2 * LANES :].T

    for i in range(blocks):
        rows = slice(i * BLOCK, (i + 1) * BLOCK)
        queries = per_head_rows(qkv_ref[rows, :LANES])
        over = spills_over(i, start)
        top = None
        for j in range(i + 1):
            scores = dot_nt(key_rows(j), queries)
            if j == i:
                scores = jnp.where(seen(j, i, start), scores, MASKED_SCORE)
            s_ref[j * BLOCK : (j + 1) * BLOCK, :] = scores
            best = jnp.max(scores, axis=0, keepdims=True)
            top = best if top is None else jnp.maximum(top, best)
        m_ref[...] = top

        if i + 1 < blocks:

            @pl.when(over)
            def _():
                scores = dot_nt(key_rows(i + 1), queries)
                scores = jnp.where(seen(i + 1, i, start), scores, MASKED_SCORE)
                s_ref[(i + 1) * BLOCK : (i + 2) * BLOCK, :] = scores
                m_ref[...] = jnp.maximum(m_ref[...], jnp.max(scores, axis=0, keepdims=True))

        top = m_ref[...]
        shift = top * SCALE
        total, mixed = None, None
        for j in range(i + 1):
            weights = jnp.exp2(s_ref[j * BLOCK : (j + 1) * BLOCK, :] * SCALE - shift)
            part_total = jnp.sum(weights, axis=0, keepdims=True)
            part_mixed = dot_nn(value_columns(j), weights.astype(bf16))
            total = part_total if total is None else total + part_total
            mixed = part_mixed if mixed is None else mixed + part_mixed
        l_ref[...] = total
        acc_ref[...] = mixed

        if i + 1 < blocks:

            @pl.when(over)
            def _():
                weights = jnp.exp2(s_ref[(i + 1) * BLOCK : (i + 2) * BLOCK, :] * SCALE - shift)
                l_ref[...] += jnp.sum(weights, axis=0, keepdims=True)
                acc_ref[...] += dot_nn(value_columns(i + 1), weights.astype(bf16))

        total = l_ref[...]
        out_ref[rows, :] = from_head_columns(acc_ref[...] / total).astype(bf16)
        lse_ref[0, i : i + 1, :] = shift + jnp.log2(total)


def attend_backward_kernel(
    start_ref, qkv_ref, out_ref, grad_ref, lse_ref, cos_ref, sin_ref, lin_ref, dq_ref, dk_ref, dv_ref
):
    start = start_ref[0]
    blocks = qkv_ref.shape[0] // BLOCK
    dk_ref[...] = jnp.zeros_like(dk_ref)
    dv_ref[...] = jnp.zeros_like(dv_ref)
    for i in range(blocks):
        rows = slice(i * BLOCK, (i + 1) * BLOCK)
        queries = per_head_rows(qkv_ref[rows, :LANES])
        grads_in = grad_ref[rows, :]
        grads = per_head_rows(grads_in)
        both = (grads_in.astype(f32) * out_ref[rows, :].astype(f32)).T
        delta = jnp.concatenate(
            [
                jnp.sum(both[:HEAD_DIM], axis=0, keepdims=True),
                jnp.sum(both[HEAD_DIM:], axis=0, keepdims=True),
            ],
            axis=1,
        )
        lse = lse_ref[0, i : i + 1, :]

        def one(j, masked):
            keys_at = slice(j * BLOCK, (j + 1) * BLOCK)
            keys = qkv_ref[keys_at, LANES : 2 * LANES]
            scores = dot_nt(keys, queries)
            weights = jnp.exp2(scores * SCALE - lse)
            if masked:
                weights = jnp.where(seen(j, i, start), weights, 0.0)
            weight_grads = dot_nt(qkv_ref[keys_at, 2 * LANES :], grads)
            score_grads = (weights * (weight_grads - delta)).astype(bf16)
            dv_ref[keys_at, :] += dot_nn(weights.astype(bf16), grads)
            dk_ref[keys_at, :] += dot_nn(score_grads, queries)
            return dot_nn(keys.T, score_grads)

        query_grads = None
        for j in range(i + 1):
            part = one(j, j == i)
            query_grads = part if query_grads is None else query_grads + part
        dq_ref[...] = query_grads

        if i + 1 < blocks:

            @pl.when(spills_over(i, start))
            def _():
                dq_ref[...] += one(i + 1, True)

        lin_ref[rows, :LANES] = turned(
            from_head_columns(dq_ref[...]) * 0.125, cos_ref[rows, :], -sin_ref[rows, :]
        ).astype(bf16)
    for i in range(blocks):
        rows = slice(i * BLOCK, (i + 1) * BLOCK)
        lin_ref[rows, LANES : 2 * LANES] = turned(
            dk_ref[rows, :] * 0.125, cos_ref[rows, :], -sin_ref[rows, :]
        ).astype(bf16)
        lin_ref[rows, 2 * LANES :] = dv_ref[rows, :].astype(bf16)


def column_block(length, width):
    return pl.BlockSpec((length, width), lambda p, s: (0, p))


def whole_block(shape):
    return pl.BlockSpec(shape, lambda p, s: (0,) * len(shape))


def attend_forward(start, lin, cosine, sine):
    length, width = lin.shape
    pairs = width // (3 * LANES)
    blocks = length // BLOCK
    flops = pairs * 2 * 2 * 2 * length * length * LANES
    return pl.pallas_call(
        attend_forward_kernel,
        grid_spec=pltpu.PrefetchScalarGridSpec(
            num_scalar_prefetch=1,
            grid=(pairs,),
            in_specs=[
                column_block(length, 3 * LANES),
                whole_block((length, LANES)),
                whole_block((length, LANES)),
            ],
            out_specs=[
                column_block(length, LANES),
                column_block(length, 3 * LANES),
                pl.BlockSpec((1, blocks, 2 * BLOCK), lambda p, s: (p, 0, 0)),
            ],
            scratch_shapes=[
                pltpu.VMEM((length, 2 * BLOCK), f32),
                pltpu.VMEM((1, 2 * BLOCK), f32),
                pltpu.VMEM((1, 2 * BLOCK), f32),
                pltpu.VMEM((LANES, 2 * BLOCK), f32),
            ],
        ),
        out_shape=[
            jax.ShapeDtypeStruct((length, pairs * LANES), bf16),
            jax.ShapeDtypeStruct((length, width), bf16),
            jax.ShapeDtypeStruct((pairs, blocks, 2 * BLOCK), f32),
        ],
        cost_estimate=pl.CostEstimate(
            flops=flops,
            bytes_accessed=length * width * 6 + length * pairs * LANES * 2,
            transcendentals=pairs * 2 * length * length // 2,
        ),
        name="attend_forward",
    )(start, lin, cosine, sine)


def attend_backward(start, qkv, out, grad, lse, cosine, sine):
    length, width = qkv.shape
    pairs = width // (3 * LANES)
    blocks = length // BLOCK
    flops = pairs * 2 * 5 * 2 * length * length * LANES
    return pl.pallas_call(
        attend_backward_kernel,
        grid_spec=pltpu.PrefetchScalarGridSpec(
            num_scalar_prefetch=1,
            grid=(pairs,),
            in_specs=[
                column_block(length, 3 * LANES),
                column_block(length, LANES),
                column_block(length, LANES),
                pl.BlockSpec((1, blocks, 2 * BLOCK), lambda p, s: (p, 0, 0)),
                whole_block((length, LANES)),
                whole_block((length, LANES)),
            ],
            out_specs=column_block(length, 3 * LANES),
            scratch_shapes=[
                pltpu.VMEM((LANES, 2 * BLOCK), f32),
                pltpu.VMEM((length, LANES), f32),
                pltpu.VMEM((length, LANES), f32),
            ],
        ),
        out_shape=jax.ShapeDtypeStruct((length, width), bf16),
        cost_estimate=pl.CostEstimate(
            flops=flops,
            bytes_accessed=length * width * 4 + length * pairs * LANES * 4,
            transcendentals=pairs * 2 * length * length // 2,
        ),
        name="attend_backward",
    )(start, qkv, out, grad, lse, cosine, sine)


def widen_kernel(place_ref, mine_ref, other_ref, out_ref):
    own = pl.program_id(0) == place_ref[0]

    @pl.when(own)
    def _():
        out_ref[...] = mine_ref[...].astype(f32)

    @pl.when(jnp.logical_not(own))
    def _():
        out_ref[...] = other_ref[...].astype(f32)


def widen_halves(place, mine, other):
    rows, width = mine.shape
    block = rows
    while block * width > 512 * 1024 and block % 32 == 0:
        block //= 2
    steps = rows // block
    return pl.pallas_call(
        widen_kernel,
        grid_spec=pltpu.PrefetchScalarGridSpec(
            num_scalar_prefetch=1,
            grid=(2, steps),
            in_specs=[
                pl.BlockSpec((block, width), lambda u, i, p: (jnp.where(u == p[0], i, 0), 0)),
                pl.BlockSpec((block, width), lambda u, i, p: (jnp.where(u == p[0], 0, i), 0)),
            ],
            out_specs=pl.BlockSpec((block, width), lambda u, i, p: (u * steps + i, 0)),
        ),
        out_shape=jax.ShapeDtypeStruct((2 * rows, width), f32),
        cost_estimate=pl.CostEstimate(
            flops=0, bytes_accessed=12 * rows * width, transcendentals=0
        ),
        name="widen_halves",
    )(place, mine, other)


def pick_heads_kernel(place_ref, q_ref, k_ref, v_ref, out_ref):
    for p in range(q_ref.shape[1] // LANES):
        for i, part_ref in enumerate((q_ref, k_ref, v_ref)):
            at = (3 * p + i) * LANES
            out_ref[:, at : at + LANES] = part_ref[:, p * LANES : (p + 1) * LANES]


def pick_heads(place, weights, heads_width, team):
    rows, full = weights[0].shape
    groups = full // (heads_width * team)
    return pl.pallas_call(
        pick_heads_kernel,
        grid_spec=pltpu.PrefetchScalarGridSpec(
            num_scalar_prefetch=1,
            grid=(groups,),
            in_specs=[pl.BlockSpec((rows, heads_width), lambda s, p: (0, s * team + p[0]))] * 3,
            out_specs=pl.BlockSpec((rows, 3 * heads_width), lambda s, p: (0, s)),
        ),
        out_shape=jax.ShapeDtypeStruct((rows, 3 * full // team), bf16),
        cost_estimate=pl.CostEstimate(
            flops=0, bytes_accessed=12 * rows * full // team, transcendentals=0
        ),
        name="pick_heads",
    )(place, *weights)


def spread_heads_kernel(place_ref, mine_ref, other_ref, q_ref, k_ref, v_ref, *, group):
    outs = (q_ref, k_ref, v_ref)
    pairs = mine_ref.shape[1] // (3 * LANES)

    def put(source_ref, place):
        for p in range(pairs):
            at = (p // group) * 2 * group * LANES + place * group * LANES + (p % group) * LANES
            for i in range(3):
                start = (3 * p + i) * LANES
                outs[i][:, at : at + LANES] = source_ref[:, start : start + LANES].astype(f32)

    for place in range(2):

        @pl.when(place_ref[0] == place)
        def _():
            put(mine_ref, place)
            put(other_ref, 1 - place)


def spread_heads(place, mine, other, heads_width):
    rows, width = mine.shape
    full = 2 * width // 3
    block = min(rows, 128)
    return pl.pallas_call(
        functools.partial(spread_heads_kernel, group=heads_width // LANES),
        grid_spec=pltpu.PrefetchScalarGridSpec(
            num_scalar_prefetch=1,
            grid=(rows // block,),
            in_specs=[pl.BlockSpec((block, width), lambda i, p: (i, 0))] * 2,
            out_specs=[pl.BlockSpec((block, full), lambda i, p: (i, 0))] * 3,
        ),
        out_shape=[jax.ShapeDtypeStruct((rows, full), f32)] * 3,
        cost_estimate=pl.CostEstimate(
            flops=0, bytes_accessed=16 * rows * full, transcendentals=0
        ),
        name="spread_heads",
    )(place, mine, other)


def line_pairs(size, stride, first, last, step):
    return [
        (i * stride + o, (i + step) * stride + o)
        for i in range(first, last + 1)
        for o in range(stride)
    ]


def line_scatter(block_of, axis, size, stride=1):
    count = size // stride
    place = lax.axis_index(axis) // stride
    total = block_of(place).astype(f32)
    if count == 1:
        return total
    last = count - 1
    up, down = block_of(last), block_of(0)
    for s in range(last):
        up = lax.ppermute(up, axis, line_pairs(size, stride, 0, s, 1))
        down = lax.ppermute(down, axis, line_pairs(size, stride, last - s, last, -1))
        if s + 1 < last:
            here_up = block_of(jnp.minimum(last - 1 - s + place, last))
            here_down = block_of(jnp.maximum(place - (last - 1 - s), 0))
            up = (up.astype(f32) + here_up.astype(f32)).astype(bf16)
            down = (down.astype(f32) + here_down.astype(f32)).astype(bf16)
    return total + up.astype(f32) + down.astype(f32)


def line_gather(value, axis, size, stride=1):
    count = size // stride
    place = lax.axis_index(axis) // stride
    rows = value.shape[0]
    last = count - 1
    ups, downs = [value], [value]
    for s in range(last):
        ups.append(lax.ppermute(ups[-1], axis, line_pairs(size, stride, s, last - 1, 1)))
        downs.append(lax.ppermute(downs[-1], axis, line_pairs(size, stride, 1, last - s, -1)))
    out = jnp.zeros((count * rows,) + value.shape[1:], value.dtype)
    out = lax.dynamic_update_slice_in_dim(out, value, place * rows, 0)
    for s in range(last):
        came = lax.select_n(place - 1 - s >= 0, downs[last - s], ups[s + 1])
        out = lax.dynamic_update_slice_in_dim(
            out, came, lax.rem(place - 1 - s + count, count) * rows, 0
        )
    return out


def together(*values):
    return lax.optimization_barrier(values)


def swap(value, axis, size, distance):
    return lax.ppermute(value, axis, [(i, i ^ distance) for i in range(size)])


def bit_orders(size):
    bits = [1 << b for b in range(size.bit_length() - 1)]
    return bits, bits[::-1]


def xor_places(order):
    places = [0]
    for bit in order:
        places += [d ^ bit for d in places]
    return places


def gather_in_order(value, place, axis, size):
    count = value.shape[0]
    half = count // 2
    out = jnp.zeros((size * count,) + value.shape[1:], value.dtype)
    for h, order in enumerate(bit_orders(size)):
        held = value[h * half : (h + 1) * half]
        for bit in order:
            held = jnp.concatenate([held, swap(held, axis, size, bit)], axis=0)
        for i, d in enumerate(xor_places(order)):
            out = lax.dynamic_update_slice_in_dim(
                out, held[i * half : (i + 1) * half], (place ^ d) * count + h * half, 0
            )
    return out


def scatter_in_order(value, place, axis, size):
    count = value.shape[0] // size
    half = count // 2
    sums = []
    for h, order in enumerate(bit_orders(size)):
        blocks = [
            lax.dynamic_slice_in_dim(value, (place ^ d) * count + h * half, half, 0)
            for d in xor_places(order)
        ]
        kept = len(blocks) // 2
        sent = jnp.concatenate(blocks[kept:], axis=0)
        total = jnp.concatenate(blocks[:kept], axis=0).astype(f32)
        for step, bit in enumerate(order[::-1]):
            if step:
                middle = total.shape[0] // 2
                sent, total = total[middle:].astype(bf16), total[:middle]
            total = total + swap(sent, axis, size, bit).astype(f32)
        sums.append(total)
    return jnp.concatenate(sums, axis=0)


def local(
    tokens,
    cotangent,
    piece_start,
    attention_gain,
    query_weight,
    key_weight,
    value_weight,
    output_weight,
    feedforward_gain,
    gate_weight,
    up_weight,
    down_weight,
):
    lengths, shards, copies = (lax.axis_size(name) for name in ("seq", "fsdp", "rep"))
    batch, span, features = tokens.shape
    hidden = gate_weight.shape[1]
    team = lengths // batch
    members = lengths * copies
    everyone = ("seq", "rep")
    own_rows = batch * span
    length = lengths * span
    part = hidden // shards
    rows = features // shards
    heads_width = features // (shards * team)
    width = features // team
    z, f, r = (lax.axis_index(name) for name in ("seq", "fsdp", "rep"))
    line = z * copies + r
    mine = lax.rem(line, team)
    local_seq = lax.rem(line // team, batch)

    def perm_in(k):
        pairs = []
        for zz in range(lengths):
            for rr in range(copies):
                j = (zz + k) % batch
                pairs.append((zz * copies + rr, (rr * batch + j) * team + zz // batch))
        return pairs

    def take_sequence(value):
        came = [
            lax.ppermute(
                lax.dynamic_index_in_dim(value, lax.rem(z + k, batch), 0, False),
                everyone,
                perm_in(k),
            )
            for k in range(batch)
        ]
        return jnp.concatenate(
            [lax.select_n(lax.rem(local_seq + batch - b, batch), *came) for b in range(batch)],
            axis=0,
        )

    def give_back(value):
        blocks = value.reshape(batch, span, features)
        came = [
            lax.ppermute(
                lax.dynamic_index_in_dim(blocks, lax.rem(local_seq + batch - k, batch), 0, False),
                everyone,
                [(b, a) for a, b in perm_in(k)],
            )
            for k in range(batch)
        ]
        return jnp.stack(
            [lax.select_n(lax.rem(j + batch * lengths - z, batch), *came) for j in range(batch)]
        )

    def team_gather(value):
        came = [value] + [swap(value, everyone, members, d) for d in range(1, team)]
        return jnp.concatenate([lax.select_n(mine ^ u, *came) for u in range(team)], axis=0)

    def team_scatter(value):
        def block(d):
            return lax.dynamic_slice_in_dim(value, (mine ^ d) * own_rows, own_rows, 0)

        total = block(0).astype(f32)
        for d in range(1, team):
            total = total + swap(block(d), everyone, members, d).astype(f32)
        return total

    def shard_gather_small(value):
        out = jnp.zeros((shards,) + value.shape, value.dtype)
        for d in range(shards):
            came = swap(value, "fsdp", shards, d) if d else value
            out = lax.dynamic_update_index_in_dim(out, came, f ^ d, 0)
        return out

    def head_columns(weight):
        split = weight.reshape(weight.shape[0], shards, team, heads_width)
        return lax.dynamic_index_in_dim(split, mine, 2, False).reshape(weight.shape[0], width)

    tokens_own = take_sequence(tokens)
    start = lax.ppermute(
        lax.dynamic_index_in_dim(piece_start, lax.rem(z, batch), 0), everyone, perm_in(0)
    )

    pairs = width // LANES
    if heads_width % LANES == 0:
        wqkv_rows = pick_heads(
            mine.astype(jnp.int32).reshape(1),
            (query_weight, key_weight, value_weight),
            heads_width,
            team,
        )
    else:
        wqkv_rows = jnp.stack(
            [
                head_columns(w).reshape(rows, pairs, LANES)
                for w in (query_weight, key_weight, value_weight)
            ],
            axis=2,
        ).reshape(rows, 3 * width)
    wqkv = gather_in_order(wqkv_rows, f, "fsdp", shards)
    wo_rows = lax.dynamic_slice_in_dim(output_weight, mine * heads_width, heads_width, 0)
    cotangent_own = take_sequence(cotangent)
    wqkv, wo_rows, gate_weight, up_weight, cotangent_own = together(
        wqkv, wo_rows, gate_weight, up_weight, cotangent_own
    )
    wo = lax.all_gather(wo_rows, "fsdp", axis=0, tiled=True)
    wo, cotangent_own = together(wo, cotangent_own)
    cot = lax.all_gather(cotangent_own, "fsdp", axis=0, tiled=True)

    slab = part // copies

    split = rows // 2
    z_low = lax.rem(z, 2)

    def column_pieces(weight, d, row):
        return lax.dynamic_slice(weight, (row, (f ^ d) * part + r * slab), (split, slab))

    fetched = [
        swap(
            jnp.stack([column_pieces(w, d, z_low * split) for w in (gate_weight, up_weight)]),
            "fsdp",
            shards,
            d,
        )
        for d in range(1, shards)
    ]

    def join_columns(i, weight, halves):
        out = jnp.zeros((shards, rows, slab), bf16)
        own = lax.dynamic_slice_in_dim(weight, f * part + r * slab, slab, 1)
        out = lax.dynamic_update_index_in_dim(out, own, f, 0)
        for low in range(2):
            for d in range(1, shards):
                piece = lax.select_n(z_low == low, halves[1][d - 1, i], halves[0][d - 1, i])
                out = lax.dynamic_update_slice(out, piece[None], (f ^ d, low * split, 0))
        out = out.reshape(features, slab)
        came = [out] + [swap(out, "rep", copies, d) for d in range(1, copies)]
        return jnp.concatenate([lax.select_n(r ^ u, *came) for u in range(copies)], axis=1)

    gains = shard_gather_small(jnp.stack([attention_gain, feedforward_gain]))
    gain_first = gains[:, 0].reshape(features).astype(f32)
    gain_second = gains[:, 1].reshape(features).astype(f32)

    half_dim = HEAD_DIM // 2
    places = jnp.arange(length, dtype=jnp.int32).astype(f32)
    frequency = ROPE_BASE ** (-jnp.arange(half_dim, dtype=f32) / half_dim)
    angles = places[:, None] * frequency[None, :]
    cos_half, sin_half = jnp.cos(angles), jnp.sin(angles)
    cosine = jnp.concatenate([cos_half] * 4, axis=1)
    sine = jnp.concatenate([-sin_half, sin_half] * 2, axis=1)

    activation = tokens_own.astype(f32)
    scale_first = lax.rsqrt(jnp.mean(activation * activation, axis=-1, keepdims=True) + NORM_EPS)
    first_own = (activation * scale_first * gain_first).astype(bf16)
    first = team_gather(first_own)
    lin = matmul(first, wqkv)
    attended, qkv, lse = attend_forward(start, lin, cosine, sine)
    attended, *fetched = together(attended, *fetched)
    fetched = jnp.stack(fetched)
    exchanged = swap(fetched, "seq", lengths, 1)
    residual = activation + team_scatter(matmul(attended, wo, bf16))
    scale_second = lax.rsqrt(jnp.mean(residual * residual, axis=-1, keepdims=True) + NORM_EPS)
    second_own = (residual * scale_second * gain_second).astype(bf16)

    gate_w = join_columns(0, gate_weight, (fetched, exchanged))
    up_w = join_columns(1, up_weight, (fetched, exchanged))
    second = gather_in_order(second_own, f, "fsdp", shards)

    inner_grad = against(cot, down_weight)
    second, inner_grad = together(second, inner_grad)
    gate = matmul(second, gate_w)
    up = matmul(second, up_w)
    sig = jax.nn.sigmoid(gate)
    silu = gate * sig
    inner = (silu * up).astype(bf16)
    gate_grad = (inner_grad * up * (sig * (1.0 + gate * (1.0 - sig)))).astype(bf16)
    up_grad = (inner_grad * silu).astype(bf16)

    tiny = rows // members

    def member_major(term):
        blocks = term.reshape(shards, members, tiny, part)
        return blocks.transpose(1, 0, 2, 3).reshape(features, part)

    down_term = outer_sum(inner, cot, bf16)
    gate_grad, up_grad, down_term = together(gate_grad, up_grad, down_term)
    second_grad_part = (against(gate_grad, gate_w) + against(up_grad, up_w)).astype(bf16)
    second_grad_part, gate_grad, up_grad, inner = together(
        second_grad_part, gate_grad, up_grad, inner
    )
    gate_term = member_major(outer_sum(second, gate_grad, bf16))
    up_term = member_major(outer_sum(second, up_grad, bf16))
    down_part = matmul(inner, down_weight, bf16)
    second_grad = scatter_in_order(second_grad_part, f, "fsdp", shards)

    def members_scatter(value):
        return lax.psum_scatter(value, everyone, scatter_dimension=0, tiled=True)

    def members_gather(value):
        return lax.all_gather(value, everyone, axis=0, tiled=False)

    gate_piece = members_scatter(gate_term)
    up_piece = members_scatter(up_term)
    down_piece = members_scatter(down_term)

    def shard_spread(piece):
        piece = piece.reshape(shards, tiny, part)
        out = jnp.zeros((tiny, hidden), bf16)
        for d in range(shards):
            came = lax.dynamic_index_in_dim(piece, f ^ d, 0, False)
            came = swap(came, "fsdp", shards, d) if d else came
            out = lax.dynamic_update_slice_in_dim(out, came, (f ^ d) * part, 1)
        return out

    gate_spread = shard_spread(gate_piece)
    up_spread = shard_spread(up_piece)

    output_rows = cotangent_own.astype(f32)
    scaled = second_grad * gain_second
    residual_grad = (
        output_rows
        + scale_second * scaled
        - residual
        * (scale_second * scale_second * scale_second)
        * jnp.mean(scaled * residual, axis=-1, keepdims=True)
    )
    gain_second_term = jnp.sum(second_grad * residual * scale_second, axis=0)
    branch_own = residual_grad.astype(bf16)
    branch_own, down_part = together(branch_own, down_part)
    layer_rows = residual + scatter_in_order(down_part, f, "fsdp", shards)
    branch = team_gather(branch_own)

    attended_grad = against(branch, wo, bf16)
    wo_term = outer_sum(attended, branch, bf16)
    attended_grad, wo_term = together(attended_grad, wo_term)
    wo_own = scatter_in_order(wo_term, f, "fsdp", shards).astype(bf16)
    lin_grad = attend_backward(start, qkv, attended, attended_grad, lse, cosine, sine)
    lin_grad, gate_spread = together(lin_grad, gate_spread)
    wqkv_term = outer_sum(first, lin_grad, bf16)
    wqkv_term, up_spread, wo_own, layer_rows = together(
        wqkv_term, up_spread, wo_own, layer_rows
    )
    layer_output = give_back(layer_rows.astype(bf16))
    wqkv_own = scatter_in_order(wqkv_term, f, "fsdp", shards).astype(bf16)
    wqkv_own, first_grad = together(wqkv_own, team_scatter(against(lin_grad, wqkv, bf16)))
    down_grad = members_gather(down_piece).reshape(part, features).astype(f32)
    gate_grad_w = members_gather(gate_spread).reshape(rows, hidden).astype(f32)
    up_grad_w = members_gather(up_spread).reshape(rows, hidden).astype(f32)

    scaled = first_grad * gain_first
    input_rows = (
        residual_grad
        + scale_first * scaled
        - activation
        * (scale_first * scale_first * scale_first)
        * jnp.mean(scaled * activation, axis=-1, keepdims=True)
    )
    gain_first_term = jnp.sum(first_grad * activation * scale_first, axis=0)
    input_gradient = give_back(input_rows.astype(bf16))

    stride = team // copies
    line = lengths // stride
    wo_rows = heads_width // line

    wo_own = wo_own.reshape(line, wo_rows, features)
    wo_own = jnp.concatenate([wo_own[:, :, t * width : (t + 1) * width] for t in range(team)], 1)
    packed = jnp.concatenate([wqkv_own, wo_own.reshape(rows, width)], axis=1)
    size = rows // line
    packed = line_scatter(
        lambda d: lax.dynamic_slice_in_dim(packed, d * size, size, 0), "seq", lengths, stride
    )
    gain_terms = jnp.stack([gain_first_term, gain_second_term])
    for axis, size in (("rep", copies), ("fsdp", shards), ("seq", lengths)):
        for bit in bit_orders(size)[0]:
            gain_terms = gain_terms + swap(gain_terms, axis, size, bit)
    packed, gain_terms = together(packed.astype(bf16), gain_terms)
    packed, gate_grad_w, up_grad_w, down_grad = together(
        line_gather(packed, "seq", lengths, stride), gate_grad_w, up_grad_w, down_grad
    )

    def unpack(value):
        out = value[:, 3 * width :].reshape(line, team, wo_rows, width)
        out = jnp.concatenate([out[:, t] for t in range(team)], axis=2)
        return value[:, : 3 * width], out.reshape(heads_width, features)

    def team_stack(value):
        came = [value] + [swap(value, everyone, members, d) for d in range(1, team)]
        return [lax.select_n(mine ^ u, *came) for u in range(team)]

    if team == 2 and heads_width % LANES == 0:
        place = mine.astype(jnp.int32).reshape(1)
        wqkv_sum, wo_sum = unpack(packed)
        wqkv_other, wo_other = unpack(swap(packed, everyone, members, 1))
        output_grad_w = widen_halves(place, wo_sum, wo_other)
        head_gradients = spread_heads(place, wqkv_sum, wqkv_other, heads_width)
    else:
        sums = [unpack(v) for v in team_stack(packed)]
        output_grad_w = jnp.concatenate([v for _, v in sums], axis=0).astype(f32)
        wqkv_all = [v.reshape(rows, pairs, 3, LANES) for v, _ in sums]

        def head_gradient(i):
            split = [v[:, :, i].reshape(rows, shards, heads_width) for v in wqkv_all]
            return jnp.stack(split, axis=2).reshape(rows, features).astype(f32)

        head_gradients = [head_gradient(i) for i in range(3)]

    gain_grads = lax.dynamic_slice_in_dim(gain_terms, f * rows, rows, 1)
    return (
        layer_output,
        input_gradient,
        gain_grads[0],
        head_gradients[0],
        head_gradients[1],
        head_gradients[2],
        output_grad_w,
        gain_grads[1],
        gate_grad_w,
        up_grad_w,
        down_grad,
    )


def solution(mesh):
    placed = (
        P(("fsdp", "rep"), "seq", None),
        P(("fsdp", "rep"), "seq", None),
        P(("fsdp", "rep")),
        P("fsdp"),
        P("fsdp", None),
        P("fsdp", None),
        P("fsdp", None),
        P("fsdp", None),
        P("fsdp"),
        P("fsdp", None),
        P("fsdp", None),
        P("fsdp", None),
    )
    return jax.shard_map(
        local,
        mesh=mesh,
        in_specs=placed,
        out_specs=(
            P(("fsdp", "rep"), "seq", None),
            P(("fsdp", "rep"), "seq", None),
            P("fsdp"),
            P("fsdp", None),
            P("fsdp", None),
            P("fsdp", None),
            P("fsdp", None),
            P("fsdp"),
            P("fsdp", None),
            P("fsdp", None),
            P("fsdp", None),
        ),
        check_vma=False,
    )
```
